32 devices in a mesh: parts: 2 (over y), mp: 4 (over z), split: 4 (over x, core).
Axes of the slice: x: 2, y: 2, z: 4, core: 2. Of those that a mesh axis runs over, the one named last changes fastest.
Arguments:
- tokens: bfloat16 [384, 5120], P(('parts', 'mp'), 'split'), parts along dimension 0, may hold values from -6 to 6
- lengths: int32 [6], P('parts'), parts along dimension 0, may hold values from 1 to 64
- teacher_gate: bfloat16 [10240, 13824], P(('parts', 'split'), 'mp'), parts along dimension 0, may hold values from -0.078125 to 0.078125
- teacher_up: bfloat16 [10240, 13824], P(('parts', 'split'), 'mp'), parts along dimension 0, may hold values from -0.078125 to 0.078125
- teacher_down: bfloat16 [27648, 5120], P(('parts', 'mp'), 'split'), parts along dimension 0, may hold values from -0.0546875 to 0.0546875
- first_gate: bfloat16 [10240, 6912], P(('parts', 'split'), 'mp'), parts along dimension 0, may hold values from -0.078125 to 0.078125
- first_up: bfloat16 [10240, 6912], P(('parts', 'split'), 'mp'), parts along dimension 0, may hold values from -0.078125 to 0.078125
- first_down: bfloat16 [13824, 5120], P(('parts', 'mp'), 'split'), parts along dimension 0, may hold values from -0.078125 to 0.078125
- second_gate: bfloat16 [10240, 5632], P(('parts', 'split'), 'mp'), parts along dimension 0, may hold values from -0.078125 to 0.078125
- second_up: bfloat16 [10240, 5632], P(('parts', 'split'), 'mp'), parts along dimension 0, may hold values from -0.078125 to 0.078125
- second_down: bfloat16 [11264, 5120], P(('parts', 'mp'), 'split'), parts along dimension 0, may hold values from -0.078125 to 0.078125
Outputs:
- grad_first_gate: bfloat16 [10240, 6912], P(('parts', 'split'), 'mp'), parts along dimension 0
- grad_first_up: bfloat16 [10240, 6912], P(('parts', 'split'), 'mp'), parts along dimension 0
- grad_first_down: bfloat16 [13824, 5120], P(('parts', 'mp'), 'split'), parts along dimension 0
- grad_second_gate: bfloat16 [10240, 5632], P(('parts', 'split'), 'mp'), parts along dimension 0
- grad_second_up: bfloat16 [10240, 5632], P(('parts', 'split'), 'mp'), parts along dimension 0
- grad_second_down: bfloat16 [11264, 5120], P(('parts', 'mp'), 'split'), parts along dimension 0
- losses: float32 [4], P('parts'), parts along dimension 0
The draws below stay inside these ranges and needn't reach their ends.
There are 2 independent parts, one for each index of `parts`. The reference program is written for one: setup_inputs(seed, part) draws one part's arguments, and reference() takes and returns one part's arrays. A program takes and returns all parts, laid end to end along the dimension named above; each array names one. Nothing has to cross between parts.
All inputs are finite; a program needn't handle non-finite values.
Results may differ from the reference program's by a relative error of at most 0.0065.
Values may be sent and summed in bfloat16 or wider, within the bound.
A program may use at most 128 MiB of HBM per device.

```python
import jax
import jax.numpy as jnp
from jax import lax

D = 5120
FT = 13824
FA = 6912
FB = 5632
LEN = 64
TOKENS = 192
SEQS = 3


def levels(key, extent, pieces, least, high):
    level = 1.0
    for axis_at, shards_of in pieces:
        draws = jax.random.uniform(jax.random.fold_in(jax.random.fold_in(key, 6), axis_at), (shards_of,), jnp.float32, least / len(pieces), high / len(pieces))
        level = level * jnp.repeat(jnp.exp(draws), extent[axis_at] // shards_of).reshape((-1,) + (1,) * (len(extent) - 1 - axis_at))
    return level


def normal_values(rng, shape, deviation, most, pieces=(), kind=jnp.bfloat16):
    drawn = deviation * jax.random.normal(rng, shape, jnp.float32)
    if pieces:
        drawn = drawn * levels(rng, shape, pieces, -0.22, 0.18)
    return jnp.clip(drawn, -most, most).astype(kind)


def setup_inputs(seed: int = 0, part: int = 0) -> dict:
    key_of = jax.random.split(jax.random.key(seed), 12)
    part_keys = jax.random.split(jax.random.fold_in(key_of[11], part), 12)
    return {
        "tokens": normal_values(part_keys[0], (TOKENS, D), 1.0, 6.0, ((0, 4), (1, 4))),
        "lengths": jax.random.randint(part_keys[1], (SEQS,), 1, LEN + 1).astype(jnp.int32),
        "teacher_gate": normal_values(part_keys[2], (D, FT), D ** -0.5, 0.078125, ((0, 4), (1, 4))),
        "teacher_up": normal_values(part_keys[3], (D, FT), D ** -0.5, 0.078125, ((0, 4), (1, 4))),
        "teacher_down": normal_values(part_keys[4], (FT, D), FT ** -0.5, 0.0546875, ((0, 4), (1, 4))),
        "first_gate": normal_values(part_keys[5], (D, FA), D ** -0.5, 0.078125, ((0, 4), (1, 4))),
        "first_up": normal_values(part_keys[6], (D, FA), D ** -0.5, 0.078125, ((0, 4), (1, 4))),
        "first_down": normal_values(part_keys[7], (FA, D), FA ** -0.5, 0.078125, ((0, 4), (1, 4))),
        "second_gate": normal_values(part_keys[8], (D, FB), D ** -0.5, 0.078125, ((0, 4), (1, 4))),
        "second_up": normal_values(part_keys[9], (D, FB), D ** -0.5, 0.078125, ((0, 4), (1, 4))),
        "second_down": normal_values(part_keys[10], (FB, D), FB ** -0.5, 0.078125, ((0, 4), (1, 4))),
    }


def contract_rows(left, right):
    return lax.dot_general(left, right, (((0,), (0,)), ((), ())), preferred_element_type=jnp.float32)


def reference(tokens, lengths, teacher_gate, teacher_up, teacher_down, first_gate, first_up, first_down, second_gate, second_up, second_down):
    def forward(gate_w, up_w):
        gate = jnp.dot(tokens, gate_w, preferred_element_type=jnp.float32)
        up = jnp.dot(tokens, up_w, preferred_element_type=jnp.float32)
        return gate, up, (jax.nn.silu(gate) * up).astype(jnp.bfloat16)

    _, _, hidden_teacher = forward(teacher_gate, teacher_up)
    gate_first, up_first, hidden_first = forward(first_gate, first_up)
    gate_second, up_second, hidden_second = forward(second_gate, second_up)
    target = jnp.dot(hidden_teacher, teacher_down, preferred_element_type=jnp.float32)
    diff_first = jnp.dot(hidden_first, first_down, preferred_element_type=jnp.float32) - target
    diff_second = jnp.dot(hidden_second, second_down, preferred_element_type=jnp.float32) - target
    position = jnp.arange(TOKENS, dtype=jnp.int32)
    seq_ids = position // LEN
    within = position - seq_ids * LEN
    limit = jnp.sum(jnp.where(seq_ids[:, None] == jnp.arange(SEQS, dtype=jnp.int32)[None, :], lengths[None, :], 0), axis=1)
    mask = (within < limit).astype(jnp.float32)[:, None]
    counted = jnp.sum(lengths).astype(jnp.float32)
    loss_first = jnp.sum(mask * diff_first * diff_first) / counted
    loss_second = jnp.sum(mask * diff_second * diff_second) / counted

    def backward(diff, gate, up, hidden, gate_w, down_w):
        cotangent = (2.0 * mask * diff / counted).astype(jnp.bfloat16)
        grad_down = contract_rows(hidden, cotangent).astype(jnp.bfloat16)
        back = lax.dot_general(cotangent, down_w, (((1,), (1,)), ((), ())), preferred_element_type=jnp.float32)
        sig = jax.nn.sigmoid(gate)
        dgate = (back * up * sig * (1.0 + gate * (1.0 - sig))).astype(jnp.bfloat16)
        dup = (back * gate * sig).astype(jnp.bfloat16)
        return contract_rows(tokens, dgate).astype(jnp.bfloat16), contract_rows(tokens, dup).astype(jnp.bfloat16), grad_down

    first_g, first_u, first_d = backward(diff_first, gate_first, up_first, hidden_first, first_gate, first_down)
    second_g, second_u, second_d = backward(diff_second, gate_second, up_second, hidden_second, second_gate, second_down)
    return first_g, first_u, first_d, second_g, second_u, second_d, jnp.stack([loss_first, loss_second])
```

```python
import functools

import jax
import jax.numpy as jnp
from jax import lax
from jax.experimental import pallas as pl
from jax.experimental.pallas import tpu as pltpu
from jax.sharding import PartitionSpec as P

MESH = pl.DeviceIdType.MESH
VMEM = pl.BlockSpec(memory_space=pltpu.VMEM)
ANY = pl.BlockSpec(memory_space=pl.ANY)
TILE = 384
GRANT = 67043328

LEN = 64


def contract_rows(left, right):
    return lax.dot_general(
        left, right, (((0,), (0,)), ((), ())), preferred_element_type=jnp.float32
    )


def valid_rows(lengths, count):
    position = jnp.arange(count, dtype=jnp.int32)
    seq_ids = position // LEN
    within = position - seq_ids * LEN
    limit = jnp.sum(
        jnp.where(
            seq_ids[:, None] == jnp.arange(lengths.shape[0], dtype=jnp.int32)[None, :],
            lengths[None, :],
            0,
        ),
        axis=1,
    )
    return (within < limit).astype(jnp.float32)[:, None]


def activate(gate, up):
    return (jax.nn.silu(gate) * up).astype(jnp.bfloat16)


def hidden_grads(back, gate, up):
    sig = jax.nn.sigmoid(gate)
    dgate = (back * up * sig * (1.0 + gate * (1.0 - sig))).astype(jnp.bfloat16)
    dup = (back * gate * sig).astype(jnp.bfloat16)
    return (dgate, dup)


def view(spot):
    return spot[0].at[spot[1]] if isinstance(spot, tuple) else spot


class Move:
    def __init__(self, *args):
        self.args = args

    def build(self):
        src, dst, send, recv, at, device = self.args
        if device is None:
            return pltpu.make_async_copy(view(src), view(dst), recv.at[at])
        return pltpu.make_async_remote_copy(
            src_ref=view(src),
            dst_ref=view(dst),
            send_sem=send.at[at],
            recv_sem=recv.at[at],
            device_id=device,
            device_id_type=MESH,
        )

    def wait(self):
        self.build().wait()

    def wait_recv(self):
        self.build().wait_recv()

    def wait_send(self):
        self.build().wait_send()


class Links:
    def __init__(self, send, recv):
        self.send, self.recv, self.count, self.made = send, recv, 0, []

    def copy(self, src, dst, device=None):
        made = Move(src, dst, self.send, self.recv, self.count, device)
        self.count += 1
        made.build().start()
        self.made.append(made)
        return made

    def settle(self, made):
        made.wait_send()
        self.made.remove(made)

    def drain(self):
        for made in self.made:
            made.wait_send()


def greet(devices):
    barrier = pltpu.get_barrier_semaphore()
    for device in devices:
        pl.semaphore_signal(barrier, inc=1, device_id=device, device_id_type=MESH)
    pl.semaphore_wait(barrier, len(devices))


def cuts(width, pieces):
    if width % 128:
        return [(0, width)]
    lanes, made, start = width // 128, [], 0
    for i in range(pieces):
        size = (lanes * (i + 1) // pieces - lanes * i // pieces) * 128
        if size:
            made.append((start, size))
        start += size
    return made


def tiles(piece, body, tile=TILE):
    start, width = piece
    full = width // tile
    if full == 1:
        body(pl.ds(start, tile))
    elif full:

        @pl.loop(0, full)
        def _(i):
            body(pl.ds(pl.multiple_of(start + i * tile, 128), tile))

    if width % tile:
        body(pl.ds(start + full * tile, width % tile))


def four_places(axis):
    me = lax.axis_index(axis)
    chip, core = me // 2, me % 2
    sib = chip * 2 + (1 - core)
    far = (1 - chip) * 2 + core
    diag = (1 - chip) * 2 + (1 - core)
    return me, sib, far, diag


class Places:
    def __init__(self, axis, count):
        self.axis, self.count = axis, count
        self.me, self.sib, self.far, self.diag = self.ids = four_places(axis)
        self.rows = [rows_at(place, count) for place in self.ids]

    def to(self, k):
        return {self.axis: self.ids[k]}


def rows_at(block, count):
    return pl.ds(pl.multiple_of(block * count, 16), count)


def part(ref, piece, rows=slice(None)):
    return ref, (rows, pl.ds(*piece))


class Unit:
    def __init__(self, links, places, refs):
        self.links, self.places = links, places
        self.snd1, self.own, self.rcv1, self.snd2, self.rcv2 = refs
        self.half = self.own.shape[0] // 2
        self.width = self.own.shape[1]
        self.first, self.second = {}, {}

    def pass_on(self, piece):
        self.first[piece] = self.links.copy(
            part(self.snd1, piece), part(self.rcv1, piece), self.places.to(1)
        )

    def multiply(self, left, weight, flip, piece):
        pair = 2 * self.half

        def body(cols):
            if flip:
                right, dims = weight[cols, :], (((1,), (1,)), ((), ()))
            else:
                right, dims = weight[:, cols], (((1,), (0,)), ((), ()))
            out = lax.dot_general(left[...], right, dims, preferred_element_type=jnp.float32)
            self.snd1[:, cols] = out[:pair].astype(self.snd1.dtype)
            self.own[:, cols] = out[pair:]

        tiles(piece, body)
        self.pass_on(piece)

    def take(self, source, piece):
        me, sib, far, diag = self.places.rows
        half = self.half
        cols = pl.ds(*piece)
        for i, rows in enumerate((diag, sib)):
            self.snd1[i * half : (i + 1) * half, cols] = source[rows, cols].astype(self.snd1.dtype)
        for i, rows in enumerate((far, me)):
            self.own[i * half : (i + 1) * half, cols] = source[rows, cols]
        self.pass_on(piece)

    def forward(self, piece):
        self.first[piece].wait_recv()
        half = self.half

        def body(cols):
            both = self.own[:half, cols] + self.rcv1[:half, cols].astype(jnp.float32)
            self.snd2[:, cols] = both.astype(jnp.bfloat16)

        tiles(piece, body)
        self.second[piece] = self.links.copy(
            part(self.snd2, piece), part(self.rcv2, piece), self.places.to(2)
        )

    def ready(self, piece):
        self.second[piece].wait_recv()

    def value(self, cols):
        half = self.half
        return (
            self.own[half:, cols]
            + self.rcv1[half:, cols].astype(jnp.float32)
            + self.rcv2[:, cols].astype(jnp.float32)
        )

    def settle(self):
        for made in (*self.first.values(), *self.second.values()):
            self.links.settle(made)


def unit_scratch(rows, width, kind=jnp.float32):
    half, pair = rows // 4, rows // 2
    return [
        pltpu.VMEM((pair, width), kind),
        pltpu.VMEM((pair, width), jnp.float32),
        pltpu.VMEM((pair, width), kind),
        pltpu.VMEM((half, width), jnp.bfloat16),
        pltpu.VMEM((half, width), jnp.bfloat16),
    ]


class Spread:
    def __init__(self, links, ref, places, piece=None, source=None):
        self.links, self.places = links, places
        piece = (0, ref.shape[1]) if piece is None else piece
        mine = part(ref, piece, places.rows[0])
        self.theirs = part(ref, piece, places.rows[2])
        source = mine if source is None else source
        self.out = links.copy(source, mine, places.to(2))
        self.side = links.copy(source, mine, places.to(1))

    def relay(self):
        self.out.wait_recv()
        self.last = self.links.copy(self.theirs, self.theirs, self.places.to(1))

    def finish(self):
        self.side.wait_recv()
        self.last.wait_recv()


def arrange(dst, src, places):
    me, sib, far, diag = places.rows
    count = places.count
    for i, rows in enumerate((diag, sib, far, me)):
        dst[i * count : (i + 1) * count, :] = src[rows, :]


def row_scale(scale, lengths):
    position = lax.broadcasted_iota(jnp.int32, scale.shape, 0)
    seq_ids = position // LEN
    within = position - seq_ids * LEN
    limit, counted = jnp.zeros(scale.shape, jnp.int32), 0
    for i in range(lengths.shape[0]):
        length = lengths[i]
        limit = jnp.where(seq_ids == i, length, limit)
        counted = counted + length
    whole = jnp.full(scale.shape, counted, jnp.int32).astype(jnp.float32)
    scale[...] = jnp.where(within < limit, 2.0 / whole, 0.0)


def layer_kernel(flips, *refs):
    refs = iter(refs)

    def take(n):
        return [next(refs) for _ in range(n)]

    (tok, lengths), weights, downs = take(2), take(6), take(3)
    kept_out, loss = take(9), take(1)[0]
    gathered, xp, xq = take(3)
    hidden, grads, cots = take(3), take(4), take(2)
    target, diff, scale, part_sums, marked = take(5)
    unit_refs = [take(5) for _ in range(6)]
    ring_refs = [take(5) for _ in range(2)]
    send, recv, wsem, dsem, osem = take(5)

    links, loads, stores = Links(send, recv), Links(None, wsem), Links(None, osem)
    places, ring = Places("split", tok.shape[0]), Places("mp", tok.shape[0])
    mine, turn = places.rows[0], ring.rows[0]
    units = [Unit(links, places, r) for r in unit_refs]
    rings = [Unit(links, ring, r) for r in ring_refs]
    layers = ((2, 3), (0, 1), (1, 2))
    pieces = {layer: cuts(units[2 * layer].width, n) for layer, n in layers}
    out = []

    def project(*wbuf):
        waits = {}
        for layer, _ in layers:
            for piece in pieces[layer]:
                for i in (2 * layer, 2 * layer + 1):
                    src, dst = weights[i], wbuf[i]
                    if piece != (0, units[i].width):
                        at = (pl.ds(*piece), slice(None))
                        at = at if flips[i] else at[::-1]
                        src, dst = (src, at), (dst, at)
                    waits[i, piece] = loads.copy(src, dst)
        row_scale(scale, lengths)
        greet([spot.to(k) for spot in (places, ring) for k in (1, 2, 3)])
        moves = Spread(links, gathered, ring, source=tok)
        gathered[turn, :] = tok[...]
        moves.relay()
        moves.finish()
        out.append(stores.copy(gathered, kept_out[0]))
        arrange(xp, gathered, places)
        behind = None
        for layer, _ in layers:
            for piece in pieces[layer]:
                for i in (2 * layer, 2 * layer + 1):
                    waits[i, piece].wait()
                    units[i].multiply(xp, wbuf[i], flips[i], piece)
                    if behind is not None:
                        units[behind[0]].forward(behind[1])
                    behind = (i, piece) if layer != 1 else None

    pl.run_scoped(project, *[pltpu.VMEM(w.shape, jnp.bfloat16) for w in weights])

    def rest(*dbuf):
        waits = {}
        drops = Links(None, dsem)
        for layer, _ in layers:
            for piece in pieces[layer]:
                rows = pl.ds(*piece)
                src, dst = (downs[layer], rows), (dbuf[layer], rows)
                waits[layer, piece] = drops.copy(src, dst)
        spreads = {}

        def activate(layer, piece):
            gate, up = units[2 * layer], units[2 * layer + 1]
            gate.ready(piece)
            up.ready(piece)

            def body(cols):
                g, u = gate.value(cols), up.value(cols)
                hidden[layer][mine, cols] = (g * jax.nn.sigmoid(g) * u).astype(
                    jnp.bfloat16
                )
                if layer < 2:
                    gate.own[gate.half :, cols] = g
                    up.own[up.half :, cols] = u

            tiles(piece, body)
            spreads[layer, piece] = Spread(links, hidden[layer], places, piece)

        wide = (0, target.shape[1])

        def project_down(layer, piece, first, dst, sign):
            spreads[layer, piece].finish()
            waits[layer, piece].wait()
            rows = pl.ds(*piece)

            def body(cols):
                out = jnp.dot(
                    hidden[layer][:, rows],
                    dbuf[layer][rows, cols],
                    preferred_element_type=jnp.float32,
                )
                if first is None:
                    dst[:, cols] += out
                elif sign:
                    dst[:, cols] = out
                else:
                    dst[:, cols] = out - first[:, cols]

            tiles(wide, body, 256)

        halves = cuts(target.shape[1], 2)
        for piece in pieces[2]:
            activate(2, piece)
        for piece in pieces[0]:
            activate(0, piece)
        for piece in pieces[1]:
            for i in (2, 3):
                units[i].forward(piece)
        for piece in pieces[2]:
            spreads[2, piece].relay()
        for n, piece in enumerate(pieces[2]):
            project_down(2, piece, None if n else target, target, n == 0)
        for piece in pieces[0]:
            spreads[0, piece].relay()
        for n, piece in enumerate(pieces[0]):
            project_down(0, piece, None if n else target, diff, False)
        out.append(stores.copy(hidden[0], kept_out[1]))
        for half in halves:
            rings[0].take(diff, half)
        for piece in pieces[1]:
            activate(1, piece)
        for half in halves:
            rings[0].forward(half)
        for piece in pieces[1]:
            spreads[1, piece].relay()
        for n, piece in enumerate(pieces[1]):
            project_down(1, piece, None if n else target, target, False)
        out.append(stores.copy(hidden[1], kept_out[2]))
        for half in halves:
            rings[1].take(target, half)

        factor = scale[turn, 0:1]
        turns, sums = [], []

        def cotangent(i):
            total_sum = 0.0
            for half in halves:
                rings[i].ready(half)
                cols = pl.ds(*half)
                total = rings[i].value(cols)
                scaled = factor * total
                cots[i][turn, cols] = scaled.astype(jnp.bfloat16)
                total_sum = total_sum + jnp.sum(scaled * total, keepdims=True)
            turns.append(Spread(links, cots[i], ring))
            sums.append(0.5 * total_sum)

        back = []
        for i in range(2):
            gate, up = units[2 * i], units[2 * i + 1]
            back.append(
                Unit(links, places, (gate.snd1, up.snd1, gate.rcv1, gate.snd2, gate.rcv2))
            )
            gate.settle()
            up.settle()
        gates = {}

        def differentiate(i):
            whole = (0, back[i].width)
            back[i].ready(whole)
            gate, up = units[2 * i], units[2 * i + 1]
            half = gate.half

            def body(cols):
                b = back[i].value(cols)
                g, u = gate.own[half:, cols], up.own[half:, cols]
                sig = jax.nn.sigmoid(g)
                dgate = b * u * sig * (1.0 + g * (1.0 - sig))
                grads[2 * i][mine, cols] = dgate.astype(jnp.bfloat16)
                grads[2 * i + 1][mine, cols] = (b * g * sig).astype(jnp.bfloat16)

            tiles(whole, body)
            gates[i] = [Spread(links, grads[2 * i + j], places) for j in range(2)]

        def back_project(i, left):
            turns[i].finish()
            out.append(stores.copy(cots[i], kept_out[3 + i]))
            arrange(left, cots[i], places)
            back[i].multiply(left, dbuf[i], True, (0, back[i].width))

        cotangent(0)
        for half in halves:
            rings[1].forward(half)
        turns[0].relay()
        cotangent(1)
        row = lax.broadcasted_iota(jnp.int32, part_sums.shape[1:], 0)
        part_sums[0] = jnp.where(row == 0, sums[0], sums[1])
        parts = [
            links.copy((part_sums, 0), (part_sums, k), ring.to(k)) for k in (1, 2, 3)
        ]
        back_project(0, xp)
        back[0].forward((0, back[0].width))
        turns[1].relay()
        differentiate(0)
        back_project(1, xq)
        back[1].forward((0, back[1].width))
        for move in parts:
            move.wait_recv()
        marked[0] = part_sums[0] + part_sums[1] + part_sums[2] + part_sums[3]
        marks = [
            links.copy((marked, 0), (marked, k), places.to(k)) for k in (1, 2, 3)
        ]
        for spread in gates[0]:
            spread.relay()
        differentiate(1)
        for mark in marks:
            mark.wait_recv()
        loss[...] = marked[0] + marked[1] + marked[2] + marked[3]
        for j, spread in enumerate(gates[0]):
            spread.finish()
            out.append(stores.copy(grads[j], kept_out[5 + j]))
        for spread in gates[1]:
            spread.relay()
        for j, spread in enumerate(gates[1]):
            spread.finish()
            out.append(stores.copy(grads[2 + j], kept_out[7 + j]))

        for made in out:
            made.wait()
        links.drain()

    pl.run_scoped(rest, *[pltpu.VMEM(d.shape, jnp.bfloat16) for d in downs])


def layer_call(mp, tokens, lengths, weights, downs, flips):
    block, depth = tokens.shape
    rows = block * mp
    widths = [d.shape[0] for d in downs]
    shape, bf16, f32 = jax.ShapeDtypeStruct, jnp.bfloat16, jnp.float32
    outs = [shape((rows, depth), bf16)]
    outs += [shape((rows, widths[i]), bf16) for i in range(2)]
    outs += [shape((rows, depth), bf16)] * 2
    outs += [shape((rows, widths[i // 2]), bf16) for i in range(4)]
    outs.append(shape((8, 128), f32))
    scratch = [pltpu.VMEM((rows, depth), bf16)] * 3
    scratch += [pltpu.VMEM((rows, w), bf16) for w in widths]
    scratch += [pltpu.VMEM((rows, widths[i // 2]), bf16) for i in range(4)]
    scratch += [pltpu.VMEM((rows, depth), bf16)] * 2
    scratch += [pltpu.VMEM((rows, depth), f32)] * 2
    scratch += [pltpu.VMEM((rows, 128), f32)]
    scratch += [pltpu.VMEM((4, 8, 128), f32)] * 2
    for i in range(6):
        scratch += unit_scratch(rows, widths[i // 2])
    for _ in range(2):
        scratch += unit_scratch(rows, depth, bf16)
    copies = 120
    scratch += [pltpu.SemaphoreType.DMA((copies,))] * 2
    scratch += [pltpu.SemaphoreType.DMA((16,))] * 3
    return pl.pallas_call(
        functools.partial(layer_kernel, flips),
        out_shape=outs,
        in_specs=[VMEM, pl.BlockSpec(memory_space=pltpu.SMEM)] + [ANY] * 9,
        out_specs=[ANY] * 9 + [VMEM],
        scratch_shapes=scratch,
        compiler_params=pltpu.CompilerParams(
            collective_id=0, has_side_effects=True, vmem_limit_bytes=GRANT
        ),
    )(tokens, lengths, *weights, *downs)


def per_device_kernels(
    mp,
    tokens,
    lengths,
    teacher_gate,
    teacher_up,
    teacher_down,
    first_gate,
    first_up,
    first_down,
    second_gate,
    second_up,
    second_down,
):
    weights, flips = [], []
    for w in (first_gate, first_up, second_gate, second_up, teacher_gate, teacher_up):
        flip = w.shape[1] % 128 != 0
        flips.append(flip)
        weights.append(w.T if flip else w)
    gathered, *rest = layer_call(
        mp, tokens, lengths, weights, (first_down, second_down, teacher_down), tuple(flips)
    )
    hidden, cots, grads_in, loss = rest[:2], rest[2:4], rest[4:8], rest[8]
    downs = [contract_rows(hidden[i], cots[i]).astype(jnp.bfloat16) for i in range(2)]
    outs = []
    for item, flip in zip(grads_in, flips):
        if flip:
            outs.append(contract_rows(item, gathered).astype(jnp.bfloat16).T)
        else:
            outs.append(contract_rows(gathered, item).astype(jnp.bfloat16))
    return outs[0], outs[1], downs[0], outs[2], outs[3], downs[1], loss[0:2, 0]


def per_device(
    tokens,
    lengths,
    teacher_gate,
    teacher_up,
    teacher_down,
    first_gate,
    first_up,
    first_down,
    second_gate,
    second_up,
    second_down,
):
    gathered = lax.all_gather(tokens, "mp", axis=0, tiled=True)
    total_rows = gathered.shape[0]

    def project(weight):
        return jnp.dot(gathered, weight, preferred_element_type=jnp.float32)

    partials = (
        project(teacher_gate),
        project(teacher_up),
        project(first_gate),
        project(first_up),
        project(second_gate),
        project(second_up),
    )
    values = lax.psum(
        (partials[0], partials[1], partials[2], partials[3], partials[4], partials[5]), "split"
    )
    hidden = (
        activate(values[0], values[1]),
        activate(values[2], values[3]),
        activate(values[4], values[5]),
    )
    target = jnp.dot(hidden[0], teacher_down, preferred_element_type=jnp.float32)
    diffs = (
        jnp.dot(hidden[1], first_down, preferred_element_type=jnp.float32) - target,
        jnp.dot(hidden[2], second_down, preferred_element_type=jnp.float32) - target,
    )
    counted = jnp.sum(lengths).astype(jnp.float32)
    summed = lax.psum((diffs[0], diffs[1]), "mp")
    mask = valid_rows(lengths, total_rows)
    partial_loss = (
        jnp.stack([jnp.sum(mask * summed[0] * summed[0]), jnp.sum(mask * summed[1] * summed[1])])
        / counted
    )
    losses = lax.psum(partial_loss, "split")
    cotangents = (
        (2.0 * mask * summed[0] / counted).astype(jnp.bfloat16),
        (2.0 * mask * summed[1] / counted).astype(jnp.bfloat16),
    )
    grad_first_down = contract_rows(hidden[1], cotangents[0]).astype(jnp.bfloat16)
    grad_second_down = contract_rows(hidden[2], cotangents[1]).astype(jnp.bfloat16)
    dims = (((1,), (1,)), ((), ()))
    backs = (
        lax.dot_general(cotangents[0], first_down, dims, preferred_element_type=jnp.float32),
        lax.dot_general(cotangents[1], second_down, dims, preferred_element_type=jnp.float32),
    )
    back_full = lax.psum((backs[0], backs[1]), "split")
    first_dg, first_du = hidden_grads(back_full[0], values[2], values[3])
    second_dg, second_du = hidden_grads(back_full[1], values[4], values[5])
    grads_in = (first_dg, first_du, second_dg, second_du)
    outputs = tuple((contract_rows(gathered, item).astype(jnp.bfloat16) for item in grads_in))
    return (
        outputs[0],
        outputs[1],
        grad_first_down,
        outputs[2],
        outputs[3],
        grad_second_down,
        losses,
    )


def run(mp, split, *args):
    rows = args[0].shape[0] * mp
    if split == 4 and mp == 4 and args[0].shape[0] % 16 == 0 and rows % 64 == 0:
        return per_device_kernels(mp, *args)
    return per_device(*args)


def solution(mesh):
    placed = (
        P(("parts", "mp"), "split"),
        P("parts"),
        P(("parts", "split"), "mp"),
        P(("parts", "split"), "mp"),
        P(("parts", "mp"), "split"),
        P(("parts", "split"), "mp"),
        P(("parts", "split"), "mp"),
        P(("parts", "mp"), "split"),
        P(("parts", "split"), "mp"),
        P(("parts", "split"), "mp"),
        P(("parts", "mp"), "split"),
    )
    return jax.shard_map(
        functools.partial(run, mesh.shape["mp"], mesh.shape["split"]),
        mesh=mesh,
        in_specs=placed,
        out_specs=(
            P(("parts", "split"), "mp"),
            P(("parts", "split"), "mp"),
            P(("parts", "mp"), "split"),
            P(("parts", "split"), "mp"),
            P(("parts", "split"), "mp"),
            P(("parts", "mp"), "split"),
            P("parts"),
        ),
        check_vma=False,
    )
```

```python
import functools

import jax
import jax.numpy as jnp
from jax import lax
from jax.experimental import pallas as pl
from jax.experimental.pallas import tpu as pltpu
from jax.sharding import PartitionSpec as P

MESH = pl.DeviceIdType.MESH
VMEM = pl.BlockSpec(memory_space=pltpu.VMEM)
ANY = pl.BlockSpec(memory_space=pl.ANY)
TILE = 384
GRANT = 67043328

LEN = 64


def contract_rows(left, right):
    return lax.dot_general(
        left, right, (((0,), (0,)), ((), ())), preferred_element_type=jnp.float32
    )


def valid_rows(lengths, count):
    position = jnp.arange(count, dtype=jnp.int32)
    seq_ids = position // LEN
    within = position - seq_ids * LEN
    limit = jnp.sum(
        jnp.where(
            seq_ids[:, None] == jnp.arange(lengths.shape[0], dtype=jnp.int32)[None, :],
            lengths[None, :],
            0,
        ),
        axis=1,
    )
    return (within < limit).astype(jnp.float32)[:, None]


def activate(gate, up):
    return (jax.nn.silu(gate) * up).astype(jnp.bfloat16)


def hidden_grads(back, gate, up):
    sig = jax.nn.sigmoid(gate)
    dgate = (back * up * sig * (1.0 + gate * (1.0 - sig))).astype(jnp.bfloat16)
    dup = (back * gate * sig).astype(jnp.bfloat16)
    return (dgate, dup)


def view(spot):
    return spot[0].at[spot[1]] if isinstance(spot, tuple) else spot


class Move:
    def __init__(self, *args):
        self.args = args

    def build(self):
        src, dst, send, recv, at, device = self.args
        if device is None:
            return pltpu.make_async_copy(view(src), view(dst), recv.at[at])
        return pltpu.make_async_remote_copy(
            src_ref=view(src),
            dst_ref=view(dst),
            send_sem=send.at[at],
            recv_sem=recv.at[at],
            device_id=device,
            device_id_type=MESH,
        )

    def wait(self):
        self.build().wait()

    def wait_recv(self):
        self.build().wait_recv()

    def wait_send(self):
        self.build().wait_send()


class Links:
    def __init__(self, send, recv):
        self.send, self.recv, self.count, self.made = send, recv, 0, []

    def copy(self, src, dst, device=None):
        made = Move(src, dst, self.send, self.recv, self.count, device)
        self.count += 1
        made.build().start()
        self.made.append(made)
        return made

    def settle(self, made):
        made.wait_send()
        self.made.remove(made)

    def drain(self):
        for made in self.made:
            made.wait_send()


def greet(devices):
    barrier = pltpu.get_barrier_semaphore()
    for device in devices:
        pl.semaphore_signal(barrier, inc=1, device_id=device, device_id_type=MESH)
    pl.semaphore_wait(barrier, len(devices))


def cuts(width, pieces):
    if width % 128:
        return [(0, width)]
    lanes, made, start = width // 128, [], 0
    for i in range(pieces):
        size = (lanes * (i + 1) // pieces - lanes * i // pieces) * 128
        if size:
            made.append((start, size))
        start += size
    return made


def tiles(piece, body, tile=TILE):
    start, width = piece
    full = width // tile
    if full == 1:
        body(pl.ds(start, tile))
    elif full:

        @pl.loop(0, full)
        def _(i):
            body(pl.ds(pl.multiple_of(start + i * tile, 128), tile))

    if width % tile:
        body(pl.ds(start + full * tile, width % tile))


def four_places(axis):
    me = lax.axis_index(axis)
    chip, core = me // 2, me % 2
    sib = chip * 2 + (1 - core)
    far = (1 - chip) * 2 + core
    diag = (1 - chip) * 2 + (1 - core)
    return me, sib, far, diag


class Places:
    def __init__(self, axis, count):
        self.axis, self.count = axis, count
        self.me, self.sib, self.far, self.diag = self.ids = four_places(axis)
        self.rows = [rows_at(place, count) for place in self.ids]

    def to(self, k):
        return {self.axis: self.ids[k]}


def rows_at(block, count):
    return pl.ds(pl.multiple_of(block * count, 16), count)


def part(ref, piece, rows=slice(None)):
    return ref, (rows, pl.ds(*piece))


class Unit:
    def __init__(self, links, places, refs):
        self.links, self.places = links, places
        self.snd1, self.own, self.rcv1, self.snd2, self.rcv2 = refs
        self.half = self.own.shape[0] // 2
        self.width = self.own.shape[1]
        self.first, self.second = {}, {}

    def pass_on(self, piece):
        self.first[piece] = self.links.copy(
            part(self.snd1, piece), part(self.rcv1, piece), self.places.to(1)
        )

    def multiply(self, left, weight, flip, piece):
        pair = 2 * self.half

        def body(cols):
            if flip:
                right, dims = weight[cols, :], (((1,), (1,)), ((), ()))
            else:
                right, dims = weight[:, cols], (((1,), (0,)), ((), ()))
            out = lax.dot_general(left[...], right, dims, preferred_element_type=jnp.float32)
            self.snd1[:, cols] = out[:pair].astype(self.snd1.dtype)
            self.own[:, cols] = out[pair:]

        tiles(piece, body)
        self.pass_on(piece)

    def take(self, source, piece):
        me, sib, far, diag = self.places.rows
        half = self.half
        cols = pl.ds(*piece)
        for i, rows in enumerate((diag, sib)):
            self.snd1[i * half : (i + 1) * half, cols] = source[rows, cols].astype(self.snd1.dtype)
        for i, rows in enumerate((far, me)):
            self.own[i * half : (i + 1) * half, cols] = source[rows, cols]
        self.pass_on(piece)

    def forward(self, piece):
        self.first[piece].wait_recv()
        half = self.half

        def body(cols):
            both = self.own[:half, cols] + self.rcv1[:half, cols].astype(jnp.float32)
            self.snd2[:, cols] = both.astype(jnp.bfloat16)

        tiles(piece, body)
        self.second[piece] = self.links.copy(
            part(self.snd2, piece), part(self.rcv2, piece), self.places.to(2)
        )

    def ready(self, piece):
        self.second[piece].wait_recv()

    def value(self, cols):
        half = self.half
        return (
            self.own[half:, cols]
            + self.rcv1[half:, cols].astype(jnp.float32)
            + self.rcv2[:, cols].astype(jnp.float32)
        )

    def settle(self):
        for made in (*self.first.values(), *self.second.values()):
            self.links.settle(made)


def unit_scratch(rows, width, kind=jnp.float32):
    half, pair = rows // 4, rows // 2
    return [
        pltpu.VMEM((pair, width), kind),
        pltpu.VMEM((pair, width), jnp.float32),
        pltpu.VMEM((pair, width), kind),
        pltpu.VMEM((half, width), jnp.bfloat16),
        pltpu.VMEM((half, width), jnp.bfloat16),
    ]


class Spread:
    def __init__(self, links, ref, places, piece=None, source=None):
        self.links, self.places = links, places
        piece = (0, ref.shape[1]) if piece is None else piece
        mine = part(ref, piece, places.rows[0])
        self.theirs = part(ref, piece, places.rows[2])
        source = mine if source is None else source
        self.out = links.copy(source, mine, places.to(2))
        self.side = links.copy(source, mine, places.to(1))

    def relay(self):
        self.out.wait_recv()
        self.last = self.links.copy(self.theirs, self.theirs, self.places.to(1))

    def finish(self):
        self.side.wait_recv()
        self.last.wait_recv()


def arrange(dst, src, places):
    me, sib, far, diag = places.rows
    count = places.count
    for i, rows in enumerate((diag, sib, far, me)):
        dst[i * count : (i + 1) * count, :] = src[rows, :]


def row_scale(scale, lengths):
    position = lax.broadcasted_iota(jnp.int32, scale.shape, 0)
    seq_ids = position // LEN
    within = position - seq_ids * LEN
    limit, counted = jnp.zeros(scale.shape, jnp.int32), 0
    for i in range(lengths.shape[0]):
        length = lengths[i]
        limit = jnp.where(seq_ids == i, length, limit)
        counted = counted + length
    whole = jnp.full(scale.shape, counted, jnp.int32).astype(jnp.float32)
    scale[...] = jnp.where(within < limit, 2.0 / whole, 0.0)


def layer_kernel(flips, *refs):
    refs = iter(refs)

    def take(n):
        return [next(refs) for _ in range(n)]

    (tok, lengths), weights, downs = take(2), take(6), take(3)
    kept_out, loss = take(9), take(1)[0]
    gathered, xp, xq = take(3)
    hidden, grads, cots = take(3), take(4), take(2)
    target, diff, scale, part_sums, marked = take(5)
    unit_refs = [take(5) for _ in range(6)]
    ring_refs = [take(5) for _ in range(2)]
    send, recv, wsem, dsem, osem = take(5)

    links, loads, stores = Links(send, recv), Links(None, wsem), Links(None, osem)
    places, ring = Places("split", tok.shape[0]), Places("mp", tok.shape[0])
    mine, turn = places.rows[0], ring.rows[0]
    units = [Unit(links, places, r) for r in unit_refs]
    rings = [Unit(links, ring, r) for r in ring_refs]
    layers = ((2, 3), (0, 1), (1, 2))
    pieces = {layer: cuts(units[2 * layer].width, n) for layer, n in layers}
    out = []

    def project(*wbuf):
        waits = {}
        for layer, _ in layers:
            for piece in pieces[layer]:
                for i in (2 * layer, 2 * layer + 1):
                    src, dst = weights[i], wbuf[i]
                    if piece != (0, units[i].width):
                        at = (pl.ds(*piece), slice(None))
                        at = at if flips[i] else at[::-1]
                        src, dst = (src, at), (dst, at)
                    waits[i, piece] = loads.copy(src, dst)
        row_scale(scale, lengths)
        greet([spot.to(k) for spot in (places, ring) for k in (1, 2, 3)])
        moves = Spread(links, gathered, ring, source=tok)
        gathered[turn, :] = tok[...]
        moves.relay()
        moves.finish()
        out.append(stores.copy(gathered, kept_out[0]))
        arrange(xp, gathered, places)
        behind = None
        for layer, _ in layers:
            for piece in pieces[layer]:
                for i in (2 * layer, 2 * layer + 1):
                    waits[i, piece].wait()
                    units[i].multiply(xp, wbuf[i], flips[i], piece)
                    if behind is not None:
                        units[behind[0]].forward(behind[1])
                    behind = (i, piece) if layer != 1 else None

    pl.run_scoped(project, *[pltpu.VMEM(w.shape, jnp.bfloat16) for w in weights])

    def rest(*dbuf):
        waits = {}
        drops = Links(None, dsem)
        for layer, _ in layers:
            for piece in pieces[layer]:
                rows = pl.ds(*piece)
                src, dst = (downs[layer], rows), (dbuf[layer], rows)
                waits[layer, piece] = drops.copy(src, dst)
        spreads = {}

        def activate(layer, piece):
            gate, up = units[2 * layer], units[2 * layer + 1]
            gate.ready(piece)
            up.ready(piece)

            def body(cols):
                g, u = gate.value(cols), up.value(cols)
                hidden[layer][mine, cols] = (g * jax.nn.sigmoid(g) * u).astype(
                    jnp.bfloat16
                )
                if layer < 2:
                    gate.own[gate.half :, cols] = g
                    up.own[up.half :, cols] = u

            tiles(piece, body)
            spreads[layer, piece] = Spread(links, hidden[layer], places, piece)

        wide = (0, target.shape[1])

        def project_down(layer, piece, first, dst, sign):
            spreads[layer, piece].finish()
            waits[layer, piece].wait()
            rows = pl.ds(*piece)

            def body(cols):
                out = jnp.dot(
                    hidden[layer][:, rows],
                    dbuf[layer][rows, cols],
                    preferred_element_type=jnp.float32,
                )
                if first is None:
                    dst[:, cols] += out
                elif sign:
                    dst[:, cols] = out
                else:
                    dst[:, cols] = out - first[:, cols]

            tiles(wide, body, 256)

        halves = cuts(target.shape[1], 2)
        for piece in pieces[2]:
            activate(2, piece)
        for piece in pieces[0]:
            activate(0, piece)
        for piece in pieces[1]:
            for i in (2, 3):
                units[i].forward(piece)
        for piece in pieces[2]:
            spreads[2, piece].relay()
        for n, piece in enumerate(pieces[2]):
            project_down(2, piece, None if n else target, target, n == 0)
        for piece in pieces[0]:
            spreads[0, piece].relay()
        for n, piece in enumerate(pieces[0]):
            project_down(0, piece, None if n else target, diff, False)
        out.append(stores.copy(hidden[0], kept_out[1]))
        for half in halves:
            rings[0].take(diff, half)
        for piece in pieces[1]:
            activate(1, piece)
        for half in halves:
            rings[0].forward(half)
        for piece in pieces[1]:
            spreads[1, piece].relay()
        for n, piece in enumerate(pieces[1]):
            project_down(1, piece, None if n else target, target, False)
        out.append(stores.copy(hidden[1], kept_out[2]))
        for half in halves:
            rings[1].take(target, half)

        factor = scale[turn, 0:1]
        turns, sums = [], []

        def cotangent(i):
            total_sum = 0.0
            for half in halves:
                rings[i].ready(half)
                cols = pl.ds(*half)
                total = rings[i].value(cols)
                scaled = factor * total
                cots[i][turn, cols] = scaled.astype(jnp.bfloat16)
                total_sum = total_sum + jnp.sum(scaled * total, keepdims=True)
            turns.append(Spread(links, cots[i], ring))
            sums.append(0.5 * total_sum)

        back = []
        for i in range(2):
            gate, up = units[2 * i], units[2 * i + 1]
            back.append(
                Unit(links, places, (gate.snd1, up.snd1, gate.rcv1, gate.snd2, gate.rcv2))
            )
            gate.settle()
            up.settle()
        gates = {}

        def differentiate(i):
            whole = (0, back[i].width)
            back[i].ready(whole)
            gate, up = units[2 * i], units[2 * i + 1]
            half = gate.half

            def body(cols):
                b = back[i].value(cols)
                g, u = gate.own[half:, cols], up.own[half:, cols]
                sig = jax.nn.sigmoid(g)
                dgate = b * u * sig * (1.0 + g * (1.0 - sig))
                grads[2 * i][mine, cols] = dgate.astype(jnp.bfloat16)
                grads[2 * i + 1][mine, cols] = (b * g * sig).astype(jnp.bfloat16)

            tiles(whole, body)
            gates[i] = [Spread(links, grads[2 * i + j], places) for j in range(2)]

        def back_project(i, left):
            turns[i].finish()
            out.append(stores.copy(cots[i], kept_out[3 + i]))
            arrange(left, cots[i], places)
            back[i].multiply(left, dbuf[i], True, (0, back[i].width))

        cotangent(0)
        for half in halves:
            rings[1].forward(half)
        turns[0].relay()
        cotangent(1)
        row = lax.broadcasted_iota(jnp.int32, part_sums.shape[1:], 0)
        part_sums[0] = jnp.where(row == 0, sums[0], sums[1])
        parts = [
            links.copy((part_sums, 0), (part_sums, k), ring.to(k)) for k in (1, 2, 3)
        ]
        back_project(0, xp)
        back[0].forward((0, back[0].width))
        turns[1].relay()
        differentiate(0)
        back_project(1, xq)
        back[1].forward((0, back[1].width))
        for move in parts:
            move.wait_recv()
        marked[0] = part_sums[0] + part_sums[1] + part_sums[2] + part_sums[3]
        marks = [
            links.copy((marked, 0), (marked, k), places.to(k)) for k in (1, 2, 3)
        ]
        for spread in gates[0]:
            spread.relay()
        differentiate(1)
        for mark in marks:
            mark.wait_recv()
        loss[...] = marked[0] + marked[1] + marked[2] + marked[3]
        for j, spread in enumerate(gates[0]):
            spread.finish()
            out.append(stores.copy(grads[j], kept_out[5 + j]))
        for spread in gates[1]:
            spread.relay()
        for j, spread in enumerate(gates[1]):
            spread.finish()
            out.append(stores.copy(grads[2 + j], kept_out[7 + j]))

        for made in out:
            made.wait()
        links.drain()

    pl.run_scoped(rest, *[pltpu.VMEM(d.shape, jnp.bfloat16) for d in downs])


def layer_call(mp, tokens, lengths, weights, downs, flips):
    block, depth = tokens.shape
    rows = block * mp
    widths = [d.shape[0] for d in downs]
    shape, bf16, f32 = jax.ShapeDtypeStruct, jnp.bfloat16, jnp.float32
    outs = [shape((rows, depth), bf16)]
    outs += [shape((rows, widths[i]), bf16) for i in range(2)]
    outs += [shape((rows, depth), bf16)] * 2
    outs += [shape((rows, widths[i // 2]), bf16) for i in range(4)]
    outs.append(shape((8, 128), f32))
    scratch = [pltpu.VMEM((rows, depth), bf16)] * 3
    scratch += [pltpu.VMEM((rows, w), bf16) for w in widths]
    scratch += [pltpu.VMEM((rows, widths[i // 2]), bf16) for i in range(4)]
    scratch += [pltpu.VMEM((rows, depth), bf16)] * 2
    scratch += [pltpu.VMEM((rows, depth), f32)] * 2
    scratch += [pltpu.VMEM((rows, 128), f32)]
    scratch += [pltpu.VMEM((4, 8, 128), f32)] * 2
    for i in range(6):
        scratch += unit_scratch(rows, widths[i // 2])
    for _ in range(2):
        scratch += unit_scratch(rows, depth, bf16)
    copies = 120
    scratch += [pltpu.SemaphoreType.DMA((copies,))] * 2
    scratch += [pltpu.SemaphoreType.DMA((16,))] * 3
    return pl.pallas_call(
        functools.partial(layer_kernel, flips),
        out_shape=outs,
        in_specs=[VMEM, pl.BlockSpec(memory_space=pltpu.SMEM)] + [ANY] * 9,
        out_specs=[ANY] * 9 + [VMEM],
        scratch_shapes=scratch,
        compiler_params=pltpu.CompilerParams(
            collective_id=0, has_side_effects=True, vmem_limit_bytes=GRANT
        ),
    )(tokens, lengths, *weights, *downs)


def gradient_kernel(jobs, *refs):
    refs = iter(refs)

    def take(n):
        return [next(refs) for _ in range(n)]

    sources, loss, outs, losses = take(9), take(1)[0], take(len(jobs)), take(1)[0]
    held, made = take(9), take(len(jobs))
    isem, osem = take(2)
    order = list(dict.fromkeys(i for job in jobs for i in job))
    loads = {i: pltpu.make_async_copy(sources[i], held[i], isem.at[i]) for i in order}
    for i in order:
        loads[i].start()
    for i in range(losses.shape[0]):
        losses[i] = loss[i, 0]
    for j, job in enumerate(jobs):
        for i in job:
            if i in loads:
                loads.pop(i).wait()
        left, right, dst = held[job[0]], held[job[1]], made[j]
        height, width = dst.shape
        step = -(-height // 256) * 128
        for start in range(0, height, step):
            rows = pl.ds(start, min(step, height - start))
            for at in range(0, width, 256):
                cols = pl.ds(at, min(256, width - at))
                dst[rows, cols] = contract_rows(left[:, rows], right[:, cols]).astype(dst.dtype)
            pltpu.make_async_copy(dst.at[rows], outs[j].at[rows], osem.at[j]).start()
    for j in range(len(jobs)):
        pltpu.make_async_copy(made[j], outs[j], osem.at[j]).wait()


def gradient_call(arrays, loss, jobs, students):
    shape = jax.ShapeDtypeStruct
    outs = [shape((arrays[a].shape[1], arrays[b].shape[1]), jnp.bfloat16) for a, b in jobs]
    smem = pl.BlockSpec(memory_space=pltpu.SMEM)
    scratch = [pltpu.VMEM(item.shape, item.dtype) for item in (*arrays, *outs)]
    scratch += [pltpu.SemaphoreType.DMA((len(arrays),)), pltpu.SemaphoreType.DMA((len(jobs),))]
    return pl.pallas_call(
        functools.partial(gradient_kernel, jobs),
        out_shape=outs + [shape((students,), jnp.float32)],
        in_specs=[ANY] * len(arrays) + [smem],
        out_specs=[ANY] * len(jobs) + [smem],
        scratch_shapes=scratch,
        compiler_params=pltpu.CompilerParams(vmem_limit_bytes=GRANT),
    )(*arrays, loss)


def per_device_kernels(
    mp,
    tokens,
    lengths,
    teacher_gate,
    teacher_up,
    teacher_down,
    first_gate,
    first_up,
    first_down,
    second_gate,
    second_up,
    second_down,
):
    weights, flips = [], []
    for w in (first_gate, first_up, second_gate, second_up, teacher_gate, teacher_up):
        flip = w.shape[1] % 128 != 0
        flips.append(flip)
        weights.append(w.T if flip else w)
    *arrays, loss = layer_call(
        mp, tokens, lengths, weights, (first_down, second_down, teacher_down), tuple(flips)
    )
    jobs = [(1, 3), (2, 4)]
    jobs += [(5 + i, 0) if flips[i] else (0, 5 + i) for i in range(4)]
    made = gradient_call(arrays, loss, tuple(jobs), 2)
    ins = [out.T if flip else out for out, flip in zip(made[2:6], flips)]
    return ins[0], ins[1], made[0], ins[2], ins[3], made[1], made[6]


def per_device(
    tokens,
    lengths,
    teacher_gate,
    teacher_up,
    teacher_down,
    first_gate,
    first_up,
    first_down,
    second_gate,
    second_up,
    second_down,
):
    gathered = lax.all_gather(tokens, "mp", axis=0, tiled=True)
    total_rows = gathered.shape[0]

    def project(weight):
        return jnp.dot(gathered, weight, preferred_element_type=jnp.float32)

    partials = (
        project(teacher_gate),
        project(teacher_up),
        project(first_gate),
        project(first_up),
        project(second_gate),
        project(second_up),
    )
    values = lax.psum(
        (partials[0], partials[1], partials[2], partials[3], partials[4], partials[5]), "split"
    )
    hidden = (
        activate(values[0], values[1]),
        activate(values[2], values[3]),
        activate(values[4], values[5]),
    )
    target = jnp.dot(hidden[0], teacher_down, preferred_element_type=jnp.float32)
    diffs = (
        jnp.dot(hidden[1], first_down, preferred_element_type=jnp.float32) - target,
        jnp.dot(hidden[2], second_down, preferred_element_type=jnp.float32) - target,
    )
    counted = jnp.sum(lengths).astype(jnp.float32)
    summed = lax.psum((diffs[0], diffs[1]), "mp")
    mask = valid_rows(lengths, total_rows)
    partial_loss = (
        jnp.stack([jnp.sum(mask * summed[0] * summed[0]), jnp.sum(mask * summed[1] * summed[1])])
        / counted
    )
    losses = lax.psum(partial_loss, "split")
    cotangents = (
        (2.0 * mask * summed[0] / counted).astype(jnp.bfloat16),
        (2.0 * mask * summed[1] / counted).astype(jnp.bfloat16),
    )
    grad_first_down = contract_rows(hidden[1], cotangents[0]).astype(jnp.bfloat16)
    grad_second_down = contract_rows(hidden[2], cotangents[1]).astype(jnp.bfloat16)
    dims = (((1,), (1,)), ((), ()))
    backs = (
        lax.dot_general(cotangents[0], first_down, dims, preferred_element_type=jnp.float32),
        lax.dot_general(cotangents[1], second_down, dims, preferred_element_type=jnp.float32),
    )
    back_full = lax.psum((backs[0], backs[1]), "split")
    first_dg, first_du = hidden_grads(back_full[0], values[2], values[3])
    second_dg, second_du = hidden_grads(back_full[1], values[4], values[5])
    grads_in = (first_dg, first_du, second_dg, second_du)
    outputs = tuple((contract_rows(gathered, item).astype(jnp.bfloat16) for item in grads_in))
    return (
        outputs[0],
        outputs[1],
        grad_first_down,
        outputs[2],
        outputs[3],
        grad_second_down,
        losses,
    )


def run(mp, split, *args):
    rows = args[0].shape[0] * mp
    if split == 4 and mp == 4 and args[0].shape[0] % 16 == 0 and rows % 64 == 0:
        return per_device_kernels(mp, *args)
    return per_device(*args)


def solution(mesh):
    placed = (
        P(("parts", "mp"), "split"),
        P("parts"),
        P(("parts", "split"), "mp"),
        P(("parts", "split"), "mp"),
        P(("parts", "mp"), "split"),
        P(("parts", "split"), "mp"),
        P(("parts", "split"), "mp"),
        P(("parts", "mp"), "split"),
        P(("parts", "split"), "mp"),
        P(("parts", "split"), "mp"),
        P(("parts", "mp"), "split"),
    )
    return jax.shard_map(
        functools.partial(run, mesh.shape["mp"], mesh.shape["split"]),
        mesh=mesh,
        in_specs=placed,
        out_specs=(
            P(("parts", "split"), "mp"),
            P(("parts", "split"), "mp"),
            P(("parts", "mp"), "split"),
            P(("parts", "split"), "mp"),
            P(("parts", "split"), "mp"),
            P(("parts", "mp"), "split"),
            P("parts"),
        ),
        check_vma=False,
    )
```

```python
import functools

import jax
import jax.numpy as jnp
from jax import lax
from jax.experimental import pallas as pl
from jax.experimental.pallas import tpu as pltpu
from jax.sharding import PartitionSpec as P

MESH = pl.DeviceIdType.MESH
VMEM = pl.BlockSpec(memory_space=pltpu.VMEM)
ANY = pl.BlockSpec(memory_space=pl.ANY)
TILE = 384
GRANT = 67043328

LEN = 64


def contract_rows(left, right):
    return lax.dot_general(
        left, right, (((0,), (0,)), ((), ())), preferred_element_type=jnp.float32
    )


def valid_rows(lengths, count):
    position = jnp.arange(count, dtype=jnp.int32)
    seq_ids = position // LEN
    within = position - seq_ids * LEN
    limit = jnp.sum(
        jnp.where(
            seq_ids[:, None] == jnp.arange(lengths.shape[0], dtype=jnp.int32)[None, :],
            lengths[None, :],
            0,
        ),
        axis=1,
    )
    return (within < limit).astype(jnp.float32)[:, None]


def activate(gate, up):
    return (jax.nn.silu(gate) * up).astype(jnp.bfloat16)


def hidden_grads(back, gate, up):
    sig = jax.nn.sigmoid(gate)
    dgate = (back * up * sig * (1.0 + gate * (1.0 - sig))).astype(jnp.bfloat16)
    dup = (back * gate * sig).astype(jnp.bfloat16)
    return (dgate, dup)


def view(spot):
    return spot[0].at[spot[1]] if isinstance(spot, tuple) else spot


class Move:
    def __init__(self, *args):
        self.args = args

    def build(self):
        src, dst, send, recv, at, device = self.args
        if device is None:
            return pltpu.make_async_copy(view(src), view(dst), recv.at[at])
        return pltpu.make_async_remote_copy(
            src_ref=view(src),
            dst_ref=view(dst),
            send_sem=send.at[at],
            recv_sem=recv.at[at],
            device_id=device,
            device_id_type=MESH,
        )

    def wait(self):
        self.build().wait()

    def wait_recv(self):
        self.build().wait_recv()

    def wait_send(self):
        self.build().wait_send()


class Links:
    def __init__(self, send, recv):
        self.send, self.recv, self.count, self.made = send, recv, 0, []

    def copy(self, src, dst, device=None):
        made = Move(src, dst, self.send, self.recv, self.count, device)
        self.count += 1
        made.build().start()
        self.made.append(made)
        return made

    def settle(self, made):
        made.wait_send()
        self.made.remove(made)

    def drain(self):
        for made in self.made:
            made.wait_send()


def greet(devices):
    barrier = pltpu.get_barrier_semaphore()
    for device in devices:
        pl.semaphore_signal(barrier, inc=1, device_id=device, device_id_type=MESH)
    pl.semaphore_wait(barrier, len(devices))


def cuts(width, shares):
    if width % 128:
        return [(0, width)]
    lanes, whole, made, taken, start = width // 128, sum(shares), [], 0, 0
    for share in shares:
        taken += share
        end = lanes * taken // whole * 128
        if end > start:
            made.append((start, end - start))
        start = end
    return made


def tiles(piece, body, tile=TILE):
    start, width = piece
    full = width // tile
    if full == 1:
        body(pl.ds(start, tile))
    elif full:

        @pl.loop(0, full)
        def _(i):
            body(pl.ds(pl.multiple_of(start + i * tile, 128), tile))

    if width % tile:
        body(pl.ds(start + full * tile, width % tile))


def four_places(axis):
    me = lax.axis_index(axis)
    chip, core = me // 2, me % 2
    sib = chip * 2 + (1 - core)
    far = (1 - chip) * 2 + core
    diag = (1 - chip) * 2 + (1 - core)
    return me, sib, far, diag


class Places:
    def __init__(self, axis, count):
        self.axis, self.count = axis, count
        self.me, self.sib, self.far, self.diag = self.ids = four_places(axis)
        self.rows = [rows_at(place, count) for place in self.ids]

    def to(self, k):
        return {self.axis: self.ids[k]}


def rows_at(block, count):
    return pl.ds(pl.multiple_of(block * count, 16), count)


def part(ref, piece, rows=slice(None)):
    return ref, (rows, pl.ds(*piece))


class Unit:
    def __init__(self, links, places, refs):
        self.links, self.places = links, places
        self.snd1, self.own, self.rcv1, self.snd2, self.rcv2 = refs
        self.half = self.own.shape[0] // 2
        self.width = self.own.shape[1]
        self.first, self.second = {}, {}

    def pass_on(self, piece):
        self.first[piece] = self.links.copy(
            part(self.snd1, piece), part(self.rcv1, piece), self.places.to(1)
        )

    def multiply(self, left, weight, flip, piece):
        pair = 2 * self.half

        def body(cols):
            if flip:
                right, dims = weight[cols, :], (((1,), (1,)), ((), ()))
            else:
                right, dims = weight[:, cols], (((1,), (0,)), ((), ()))
            out = lax.dot_general(left[...], right, dims, preferred_element_type=jnp.float32)
            self.snd1[:, cols] = out[:pair].astype(self.snd1.dtype)
            self.own[:, cols] = out[pair:]

        tiles(piece, body)
        self.pass_on(piece)

    def take(self, source, piece):
        me, sib, far, diag = self.places.rows
        half = self.half
        cols = pl.ds(*piece)
        for i, rows in enumerate((diag, sib)):
            self.snd1[i * half : (i + 1) * half, cols] = source[rows, cols].astype(self.snd1.dtype)
        for i, rows in enumerate((far, me)):
            self.own[i * half : (i + 1) * half, cols] = source[rows, cols]
        self.pass_on(piece)

    def forward(self, piece):
        self.first[piece].wait_recv()
        half = self.half

        def body(cols):
            both = self.own[:half, cols] + self.rcv1[:half, cols].astype(jnp.float32)
            self.snd2[:, cols] = both.astype(jnp.bfloat16)

        tiles(piece, body)
        self.second[piece] = self.links.copy(
            part(self.snd2, piece), part(self.rcv2, piece), self.places.to(2)
        )

    def ready(self, piece):
        self.second[piece].wait_recv()

    def value(self, cols):
        half = self.half
        return (
            self.own[half:, cols]
            + self.rcv1[half:, cols].astype(jnp.float32)
            + self.rcv2[:, cols].astype(jnp.float32)
        )

    def settle(self):
        for made in (*self.first.values(), *self.second.values()):
            self.links.settle(made)


class Exchange(Unit):
    def __init__(self, links, places, refs):
        super().__init__(links, places, (*refs[:3], None, None))
        self.snd2, self.rcv2 = refs[3], refs[4]

    def forward(self, piece):
        self.first[piece].wait_recv()
        half = self.half

        def body(cols):
            for k in range(2):
                rows = slice(k * half, (k + 1) * half)
                both = self.own[rows, cols] + self.rcv1[rows, cols]
                self.own[rows, cols] = both
                self.snd2[k][:, cols] = both.astype(jnp.bfloat16)

        tiles(piece, body)
        self.second[piece] = [
            self.links.copy(part(self.snd2[k], piece), part(self.rcv2[1 - k], piece), self.places.to(2))
            for k in range(2)
        ]

    def ready(self, piece):
        for made in self.second[piece]:
            made.wait_recv()

    def value(self, k, cols):
        rows = slice(k * self.half, (k + 1) * self.half)
        return self.own[rows, cols] + self.rcv2[k][:, cols].astype(jnp.float32)


def unit_scratch(rows, width, kind=jnp.float32):
    half, pair = rows // 4, rows // 2
    return [
        pltpu.VMEM((pair, width), kind),
        pltpu.VMEM((pair, width), jnp.float32),
        pltpu.VMEM((pair, width), kind),
        pltpu.VMEM((half, width), jnp.bfloat16),
        pltpu.VMEM((half, width), jnp.bfloat16),
    ]


class Spread:
    def __init__(self, links, ref, places, piece=None, source=None):
        self.links, self.places = links, places
        piece = (0, ref.shape[1]) if piece is None else piece
        mine = part(ref, piece, places.rows[0])
        self.theirs = part(ref, piece, places.rows[2])
        source = mine if source is None else source
        self.out = links.copy(source, mine, places.to(2))
        self.side = links.copy(source, mine, places.to(1))

    def relay(self):
        self.out.wait_recv()
        self.last = self.links.copy(self.theirs, self.theirs, self.places.to(1))

    def finish(self):
        self.side.wait_recv()
        self.last.wait_recv()


def arrange(dst, src, places):
    me, sib, far, diag = places.rows
    count = places.count
    for i, rows in enumerate((diag, sib, far, me)):
        dst[i * count : (i + 1) * count, :] = src[rows, :]


def row_scale(scale, lengths):
    position = lax.broadcasted_iota(jnp.int32, scale.shape, 0)
    seq_ids = position // LEN
    within = position - seq_ids * LEN
    limit, counted = jnp.zeros(scale.shape, jnp.int32), 0
    for i in range(lengths.shape[0]):
        length = lengths[i]
        limit = jnp.where(seq_ids == i, length, limit)
        counted = counted + length
    whole = jnp.full(scale.shape, counted, jnp.int32).astype(jnp.float32)
    scale[...] = jnp.where(within < limit, 2.0 / whole, 0.0)


def layer_kernel(flips, *refs):
    refs = iter(refs)

    def take(n):
        return [next(refs) for _ in range(n)]

    (tok, lengths), weights, downs = take(2), take(6), take(3)
    kept_out, loss = take(9), take(1)[0]
    gathered, xp, xq = take(3)
    hidden, grads, cots = take(3), take(4), take(2)
    near, away = take(4), take(4)
    target, diff, scale, part_sums, marked = take(5)
    unit_refs = [take(5) for _ in range(6)]
    ring_refs = [take(5) for _ in range(2)]
    send, recv, wsem, dsem, osem = take(5)

    links, loads, stores = Links(send, recv), Links(None, wsem), Links(None, osem)
    places, ring = Places("split", tok.shape[0]), Places("mp", tok.shape[0])
    mine, turn = places.rows[0], ring.rows[0]
    units = [Unit(links, places, r) for r in unit_refs]
    rings = [Unit(links, ring, r) for r in ring_refs]
    layers = ((2, (1, 2, 3, 3)), (0, (1,)), (1, (6, 5)))
    pieces = {layer: cuts(units[2 * layer].width, n) for layer, n in layers}
    out = []

    def project(*wbuf):
        waits = {}
        for layer, _ in layers:
            for piece in pieces[layer]:
                for i in (2 * layer, 2 * layer + 1):
                    src, dst = weights[i], wbuf[i]
                    if piece != (0, units[i].width):
                        at = (pl.ds(*piece), slice(None))
                        at = at if flips[i] else at[::-1]
                        src, dst = (src, at), (dst, at)
                    waits[i, piece] = loads.copy(src, dst)
        row_scale(scale, lengths)
        greet([spot.to(k) for spot in (places, ring) for k in (1, 2, 3)])
        moves = Spread(links, gathered, ring, source=tok)
        gathered[turn, :] = tok[...]
        moves.relay()
        moves.finish()
        out.append(stores.copy(gathered, kept_out[0]))
        arrange(xp, gathered, places)
        behind = None
        for layer, _ in layers:
            for piece in pieces[layer]:
                for i in (2 * layer, 2 * layer + 1):
                    waits[i, piece].wait()
                    units[i].multiply(xp, wbuf[i], flips[i], piece)
                    if behind is not None:
                        units[behind[0]].forward(behind[1])
                    behind = (i, piece) if layer != 1 else None

    pl.run_scoped(project, *[pltpu.VMEM(w.shape, jnp.bfloat16) for w in weights])

    def rest(*dbuf):
        waits = {}
        drops = Links(None, dsem)
        for layer, _ in layers:
            for piece in pieces[layer]:
                rows = pl.ds(*piece)
                src, dst = (downs[layer], rows), (dbuf[layer], rows)
                waits[layer, piece] = drops.copy(src, dst)
        spreads = {}

        def activate(layer, piece):
            gate, up = units[2 * layer], units[2 * layer + 1]
            gate.ready(piece)
            up.ready(piece)

            def body(cols):
                g, u = gate.value(cols), up.value(cols)
                sig = jax.nn.sigmoid(g)
                slope = g * sig
                hidden[layer][mine, cols] = (slope * u).astype(jnp.bfloat16)
                if layer < 2:
                    bend = u * sig * (1.0 + g * (1.0 - sig))
                    gate.own[gate.half :, cols] = bend
                    up.own[up.half :, cols] = slope
                    near[2 * layer][:, cols] = bend.astype(jnp.bfloat16)
                    near[2 * layer + 1][:, cols] = slope.astype(jnp.bfloat16)

            tiles(piece, body)
            spreads[layer, piece] = Spread(links, hidden[layer], places, piece)

        wide = (0, target.shape[1])

        def project_down(layer, piece, first, dst, sign):
            spreads[layer, piece].finish()
            waits[layer, piece].wait()
            rows = pl.ds(*piece)

            def body(cols):
                out = jnp.dot(
                    hidden[layer][:, rows],
                    dbuf[layer][rows, cols],
                    preferred_element_type=jnp.float32,
                )
                if first is None:
                    dst[:, cols] += out
                elif sign:
                    dst[:, cols] = out
                else:
                    dst[:, cols] = out - first[:, cols]

            tiles(wide, body, 256)

        halves = cuts(target.shape[1], (1, 1))
        for piece in pieces[2]:
            activate(2, piece)
        for piece in pieces[0]:
            activate(0, piece)
        for piece in pieces[1]:
            for i in (2, 3):
                units[i].forward(piece)
        for piece in pieces[2]:
            spreads[2, piece].relay()
        for n, piece in enumerate(pieces[2]):
            project_down(2, piece, None if n else target, target, n == 0)
        for piece in pieces[0]:
            spreads[0, piece].relay()
        for n, piece in enumerate(pieces[0]):
            project_down(0, piece, None if n else target, diff, False)
        out.append(stores.copy(hidden[0], kept_out[1]))
        for half in halves:
            rings[0].take(diff, half)
        for piece in pieces[1]:
            activate(1, piece)
        lent = [links.copy(near[i], away[i], places.to(2)) for i in range(4)]
        for half in halves:
            rings[0].forward(half)
        for piece in pieces[1]:
            spreads[1, piece].relay()
        for n, piece in enumerate(pieces[1]):
            project_down(1, piece, None if n else target, target, False)
        out.append(stores.copy(hidden[1], kept_out[2]))
        for half in halves:
            rings[1].take(target, half)

        factor = scale[turn, 0:1]
        turns, sums = [], []

        def cotangent(i):
            total_sum = 0.0
            for half in halves:
                rings[i].ready(half)
                cols = pl.ds(*half)
                total = rings[i].value(cols)
                scaled = factor * total
                cots[i][turn, cols] = scaled.astype(jnp.bfloat16)
                total_sum = total_sum + jnp.sum(scaled * total, keepdims=True)
            turns.append(Spread(links, cots[i], ring))
            sums.append(0.5 * total_sum)

        back, parcels = [], [[], []]
        for i in range(2):
            gate, up = units[2 * i], units[2 * i + 1]
            pair = ((up.snd2, gate.snd2), (up.rcv2, gate.rcv2))
            back.append(Exchange(links, places, (gate.snd1, up.snd1, gate.rcv1, *pair)))
            gate.settle()
            up.settle()

        def differentiate(i, piece):
            back[i].ready(piece)
            half = back[i].half

            def body(cols):
                for k, rows in enumerate((places.rows[2], mine)):
                    value = back[i].value(k, cols)
                    for j in range(2):
                        factor = units[2 * i + j].own[half:, cols] if k else away[2 * i + j][:, cols]
                        out = value * factor.astype(jnp.float32)
                        grads[2 * i + j][rows, cols] = out.astype(jnp.bfloat16)

            tiles(piece, body)
            for j in range(2):
                for rows in (places.rows[2], mine):
                    spot = part(grads[2 * i + j], piece, rows)
                    parcels[i].append(links.copy(spot, spot, places.to(1)))

        def collect(i):
            for made in parcels[i]:
                made.wait_recv()
            for j in range(2):
                out.append(stores.copy(grads[2 * i + j], kept_out[5 + 2 * i + j]))

        def back_project(i, left):
            turns[i].finish()
            out.append(stores.copy(cots[i], kept_out[3 + i]))
            arrange(left, cots[i], places)
            for piece in pieces[i]:
                back[i].multiply(left, dbuf[i], True, piece)

        cotangent(0)
        for half in halves:
            rings[1].forward(half)
        turns[0].relay()
        cotangent(1)
        row = lax.broadcasted_iota(jnp.int32, part_sums.shape[1:], 0)
        part_sums[0] = jnp.where(row == 0, sums[0], sums[1])
        parts = [
            links.copy((part_sums, 0), (part_sums, k), ring.to(k)) for k in (1, 2, 3)
        ]
        back_project(0, xp)
        for piece in pieces[0]:
            back[0].forward(piece)
        turns[1].relay()
        back_project(1, xq)
        for piece in pieces[1]:
            back[1].forward(piece)
        for made in lent:
            made.wait_recv()
        for piece in pieces[0]:
            differentiate(0, piece)
        for move in parts:
            move.wait_recv()
        marked[0] = part_sums[0] + part_sums[1] + part_sums[2] + part_sums[3]
        marks = [
            links.copy((marked, 0), (marked, k), places.to(k)) for k in (1, 2, 3)
        ]
        collect(0)
        for piece in pieces[1]:
            differentiate(1, piece)
        for mark in marks:
            mark.wait_recv()
        loss[...] = marked[0] + marked[1] + marked[2] + marked[3]
        collect(1)
        for made in out:
            made.wait()
        links.drain()

    pl.run_scoped(rest, *[pltpu.VMEM(d.shape, jnp.bfloat16) for d in downs])


def layer_call(mp, tokens, lengths, weights, downs, flips):
    block, depth = tokens.shape
    rows = block * mp
    widths = [d.shape[0] for d in downs]
    shape, bf16, f32 = jax.ShapeDtypeStruct, jnp.bfloat16, jnp.float32
    outs = [shape((rows, depth), bf16)]
    outs += [shape((rows, widths[i]), bf16) for i in range(2)]
    outs += [shape((rows, depth), bf16)] * 2
    outs += [shape((rows, widths[i // 2]), bf16) for i in range(4)]
    outs.append(shape((8, 128), f32))
    scratch = [pltpu.VMEM((rows, depth), bf16)] * 3
    scratch += [pltpu.VMEM((rows, w), bf16) for w in widths]
    scratch += [pltpu.VMEM((rows, widths[i // 2]), bf16) for i in range(4)]
    scratch += [pltpu.VMEM((rows, depth), bf16)] * 2
    scratch += [pltpu.VMEM((block, widths[i // 2]), bf16) for i in range(4)] * 2
    scratch += [pltpu.VMEM((rows, depth), f32)] * 2
    scratch += [pltpu.VMEM((rows, 128), f32)]
    scratch += [pltpu.VMEM((4, 8, 128), f32)] * 2
    for i in range(6):
        scratch += unit_scratch(rows, widths[i // 2])
    for _ in range(2):
        scratch += unit_scratch(rows, depth, bf16)
    copies = 120
    scratch += [pltpu.SemaphoreType.DMA((copies,))] * 2
    scratch += [pltpu.SemaphoreType.DMA((16,))] * 3
    return pl.pallas_call(
        functools.partial(layer_kernel, flips),
        out_shape=outs,
        in_specs=[VMEM, pl.BlockSpec(memory_space=pltpu.SMEM)] + [ANY] * 9,
        out_specs=[ANY] * 9 + [VMEM],
        scratch_shapes=scratch,
        compiler_params=pltpu.CompilerParams(
            collective_id=0, has_side_effects=True, vmem_limit_bytes=GRANT
        ),
    )(tokens, lengths, *weights, *downs)


def gradient_kernel(jobs, *refs):
    refs = iter(refs)

    def take(n):
        return [next(refs) for _ in range(n)]

    sources, loss, outs, losses = take(9), take(1)[0], take(len(jobs)), take(1)[0]
    held, made = take(9), take(len(jobs))
    isem, osem = take(2)
    order = list(dict.fromkeys(i for job in jobs for i in job))
    loads = {i: pltpu.make_async_copy(sources[i], held[i], isem.at[i]) for i in order}
    for i in order:
        loads[i].start()
    for i in range(losses.shape[0]):
        losses[i] = loss[i, 0]
    for j, job in enumerate(jobs):
        for i in job:
            if i in loads:
                loads.pop(i).wait()
        left, right, dst = held[job[0]], held[job[1]], made[j]
        height, width = dst.shape
        step = -(-height // 256) * 128
        for start in range(0, height, step):
            rows = pl.ds(start, min(step, height - start))
            for at in range(0, width, 256):
                cols = pl.ds(at, min(256, width - at))
                dst[rows, cols] = contract_rows(left[:, rows], right[:, cols]).astype(dst.dtype)
            pltpu.make_async_copy(dst.at[rows], outs[j].at[rows], osem.at[j]).start()
    for j in range(len(jobs)):
        pltpu.make_async_copy(made[j], outs[j], osem.at[j]).wait()


def gradient_call(arrays, loss, jobs, students):
    shape = jax.ShapeDtypeStruct
    outs = [shape((arrays[a].shape[1], arrays[b].shape[1]), jnp.bfloat16) for a, b in jobs]
    smem = pl.BlockSpec(memory_space=pltpu.SMEM)
    scratch = [pltpu.VMEM(item.shape, item.dtype) for item in (*arrays, *outs)]
    scratch += [pltpu.SemaphoreType.DMA((len(arrays),)), pltpu.SemaphoreType.DMA((len(jobs),))]
    return pl.pallas_call(
        functools.partial(gradient_kernel, jobs),
        out_shape=outs + [shape((students,), jnp.float32)],
        in_specs=[ANY] * len(arrays) + [smem],
        out_specs=[ANY] * len(jobs) + [smem],
        scratch_shapes=scratch,
        compiler_params=pltpu.CompilerParams(vmem_limit_bytes=GRANT),
    )(*arrays, loss)


def per_device_kernels(
    mp,
    tokens,
    lengths,
    teacher_gate,
    teacher_up,
    teacher_down,
    first_gate,
    first_up,
    first_down,
    second_gate,
    second_up,
    second_down,
):
    weights, flips = [], []
    for w in (first_gate, first_up, second_gate, second_up, teacher_gate, teacher_up):
        flip = w.shape[1] % 128 != 0
        flips.append(flip)
        weights.append(w.T if flip else w)
    *arrays, loss = layer_call(
        mp, tokens, lengths, weights, (first_down, second_down, teacher_down), tuple(flips)
    )
    jobs = [(1, 3), (2, 4)]
    jobs += [(5 + i, 0) if flips[i] else (0, 5 + i) for i in range(4)]
    made = gradient_call(arrays, loss, tuple(jobs), 2)
    ins = [out.T if flip else out for out, flip in zip(made[2:6], flips)]
    return ins[0], ins[1], made[0], ins[2], ins[3], made[1], made[6]


def per_device(
    tokens,
    lengths,
    teacher_gate,
    teacher_up,
    teacher_down,
    first_gate,
    first_up,
    first_down,
    second_gate,
    second_up,
    second_down,
):
    gathered = lax.all_gather(tokens, "mp", axis=0, tiled=True)
    total_rows = gathered.shape[0]

    def project(weight):
        return jnp.dot(gathered, weight, preferred_element_type=jnp.float32)

    partials = (
        project(teacher_gate),
        project(teacher_up),
        project(first_gate),
        project(first_up),
        project(second_gate),
        project(second_up),
    )
    values = lax.psum(
        (partials[0], partials[1], partials[2], partials[3], partials[4], partials[5]), "split"
    )
    hidden = (
        activate(values[0], values[1]),
        activate(values[2], values[3]),
        activate(values[4], values[5]),
    )
    target = jnp.dot(hidden[0], teacher_down, preferred_element_type=jnp.float32)
    diffs = (
        jnp.dot(hidden[1], first_down, preferred_element_type=jnp.float32) - target,
        jnp.dot(hidden[2], second_down, preferred_element_type=jnp.float32) - target,
    )
    counted = jnp.sum(lengths).astype(jnp.float32)
    summed = lax.psum((diffs[0], diffs[1]), "mp")
    mask = valid_rows(lengths, total_rows)
    partial_loss = (
        jnp.stack([jnp.sum(mask * summed[0] * summed[0]), jnp.sum(mask * summed[1] * summed[1])])
        / counted
    )
    losses = lax.psum(partial_loss, "split")
    cotangents = (
        (2.0 * mask * summed[0] / counted).astype(jnp.bfloat16),
        (2.0 * mask * summed[1] / counted).astype(jnp.bfloat16),
    )
    grad_first_down = contract_rows(hidden[1], cotangents[0]).astype(jnp.bfloat16)
    grad_second_down = contract_rows(hidden[2], cotangents[1]).astype(jnp.bfloat16)
    dims = (((1,), (1,)), ((), ()))
    backs = (
        lax.dot_general(cotangents[0], first_down, dims, preferred_element_type=jnp.float32),
        lax.dot_general(cotangents[1], second_down, dims, preferred_element_type=jnp.float32),
    )
    back_full = lax.psum((backs[0], backs[1]), "split")
    first_dg, first_du = hidden_grads(back_full[0], values[2], values[3])
    second_dg, second_du = hidden_grads(back_full[1], values[4], values[5])
    grads_in = (first_dg, first_du, second_dg, second_du)
    outputs = tuple((contract_rows(gathered, item).astype(jnp.bfloat16) for item in grads_in))
    return (
        outputs[0],
        outputs[1],
        grad_first_down,
        outputs[2],
        outputs[3],
        grad_second_down,
        losses,
    )


def run(mp, split, *args):
    rows = args[0].shape[0] * mp
    if split == 4 and mp == 4 and args[0].shape[0] % 16 == 0 and rows % 64 == 0:
        return per_device_kernels(mp, *args)
    return per_device(*args)


def solution(mesh):
    placed = (
        P(("parts", "mp"), "split"),
        P("parts"),
        P(("parts", "split"), "mp"),
        P(("parts", "split"), "mp"),
        P(("parts", "mp"), "split"),
        P(("parts", "split"), "mp"),
        P(("parts", "split"), "mp"),
        P(("parts", "mp"), "split"),
        P(("parts", "split"), "mp"),
        P(("parts", "split"), "mp"),
        P(("parts", "mp"), "split"),
    )
    return jax.shard_map(
        functools.partial(run, mesh.shape["mp"], mesh.shape["split"]),
        mesh=mesh,
        in_specs=placed,
        out_specs=(
            P(("parts", "split"), "mp"),
            P(("parts", "split"), "mp"),
            P(("parts", "mp"), "split"),
            P(("parts", "split"), "mp"),
            P(("parts", "split"), "mp"),
            P(("parts", "mp"), "split"),
            P("parts"),
        ),
        check_vma=False,
    )
```

```python
import functools

import jax
import jax.numpy as jnp
from jax import lax
from jax.experimental import pallas as pl
from jax.experimental.pallas import tpu as pltpu
from jax.sharding import PartitionSpec as P

MESH = pl.DeviceIdType.MESH
VMEM = pl.BlockSpec(memory_space=pltpu.VMEM)
ANY = pl.BlockSpec(memory_space=pl.ANY)
TILE = 384
GRANT = 67043328

LEN = 64


def contract_rows(left, right):
    return lax.dot_general(
        left, right, (((0,), (0,)), ((), ())), preferred_element_type=jnp.float32
    )


def valid_rows(lengths, count):
    position = jnp.arange(count, dtype=jnp.int32)
    seq_ids = position // LEN
    within = position - seq_ids * LEN
    limit = jnp.sum(
        jnp.where(
            seq_ids[:, None] == jnp.arange(lengths.shape[0], dtype=jnp.int32)[None, :],
            lengths[None, :],
            0,
        ),
        axis=1,
    )
    return (within < limit).astype(jnp.float32)[:, None]


def activate(gate, up):
    return (jax.nn.silu(gate) * up).astype(jnp.bfloat16)


def hidden_grads(back, gate, up):
    sig = jax.nn.sigmoid(gate)
    dgate = (back * up * sig * (1.0 + gate * (1.0 - sig))).astype(jnp.bfloat16)
    dup = (back * gate * sig).astype(jnp.bfloat16)
    return (dgate, dup)


def view(spot):
    return spot[0].at[spot[1]] if isinstance(spot, tuple) else spot


class Move:
    def __init__(self, *args):
        self.args = args

    def build(self):
        src, dst, send, recv, at, land, device = self.args
        if device is None:
            return pltpu.make_async_copy(view(src), view(dst), recv.at[land])
        return pltpu.make_async_remote_copy(
            src_ref=view(src),
            dst_ref=view(dst),
            send_sem=send.at[at],
            recv_sem=recv.at[land],
            device_id=device,
            device_id_type=MESH,
        )

    def wait(self):
        self.build().wait()

    def wait_recv(self):
        self.build().wait_recv()

    def wait_send(self):
        self.build().wait_send()


class Links:
    def __init__(self, send, recv):
        self.send, self.recv, self.count, self.made = send, recv, 0, []

    def copy(self, src, dst, device=None):
        at = self.reserve(1)
        made = Move(src, dst, self.send, self.recv, at, at, device)
        made.build().start()
        self.made.append(made)
        return made

    def reserve(self, count):
        at = self.count
        self.count += count
        return at

    def settle(self, made):
        made.wait_send()
        self.made.remove(made)

    def drain(self):
        for made in self.made:
            made.wait_send()


def greet(devices):
    barrier = pltpu.get_barrier_semaphore()
    for device in devices:
        pl.semaphore_signal(barrier, inc=1, device_id=device, device_id_type=MESH)
    pl.semaphore_wait(barrier, len(devices))


def cuts(width, shares):
    if width % 128:
        return [(0, width)]
    lanes, whole, made, taken, start = width // 128, sum(shares), [], 0, 0
    for share in shares:
        taken += share
        end = lanes * taken // whole * 128
        if end > start:
            made.append((start, end - start))
        start = end
    return made


def tiles(piece, body, tile=TILE):
    start, width = piece
    full = width // tile
    if full == 1:
        body(pl.ds(start, tile))
    elif full:

        @pl.loop(0, full)
        def _(i):
            body(pl.ds(pl.multiple_of(start + i * tile, 128), tile))

    if width % tile:
        body(pl.ds(start + full * tile, width % tile))


def four_places(axis):
    me = lax.axis_index(axis)
    chip, core = me // 2, me % 2
    sib = chip * 2 + (1 - core)
    far = (1 - chip) * 2 + core
    diag = (1 - chip) * 2 + (1 - core)
    return me, sib, far, diag


class Places:
    def __init__(self, axis, count):
        self.axis, self.count = axis, count
        self.me, self.sib, self.far, self.diag = self.ids = four_places(axis)
        self.rows = [rows_at(place, count) for place in self.ids]

    def to(self, k):
        return {self.axis: self.ids[k]}


def rows_at(block, count):
    return pl.ds(pl.multiple_of(block * count, 16), count)


def part(ref, piece, rows=slice(None)):
    return ref, (rows, pl.ds(*piece))


class Unit:
    def __init__(self, links, places, refs):
        self.links, self.places = links, places
        self.snd1, self.own, self.rcv1, self.snd2, self.rcv2 = refs
        self.half = self.own.shape[0] // 2
        self.width = self.own.shape[1]
        self.first, self.second = {}, {}

    def pass_on(self, piece):
        self.first[piece] = self.links.copy(
            part(self.snd1, piece), part(self.rcv1, piece), self.places.to(1)
        )

    def multiply(self, left, weight, flip, piece):
        pair = 2 * self.half

        def body(cols):
            if flip:
                right, dims = weight[cols, :], (((1,), (1,)), ((), ()))
            else:
                right, dims = weight[:, cols], (((1,), (0,)), ((), ()))
            out = lax.dot_general(left[...], right, dims, preferred_element_type=jnp.float32)
            self.snd1[:, cols] = out[:pair].astype(self.snd1.dtype)
            self.own[:, cols] = out[pair:]

        tiles(piece, body)
        self.pass_on(piece)

    def forward(self, piece):
        self.first[piece].wait_recv()
        half = self.half

        def body(cols):
            both = self.own[:half, cols] + self.rcv1[:half, cols].astype(jnp.float32)
            self.snd2[:, cols] = both.astype(jnp.bfloat16)

        tiles(piece, body)
        self.second[piece] = self.links.copy(
            part(self.snd2, piece), part(self.rcv2, piece), self.places.to(2)
        )

    def ready(self, piece):
        self.second[piece].wait_recv()

    def value(self, cols):
        half = self.half
        return (
            self.own[half:, cols]
            + self.rcv1[half:, cols].astype(jnp.float32)
            + self.rcv2[:, cols].astype(jnp.float32)
        )

    def settle(self):
        for made in (*self.first.values(), *self.second.values()):
            self.links.settle(made)


class Exchange(Unit):
    def __init__(self, links, places, refs):
        super().__init__(links, places, (*refs[:3], None, None))
        self.snd2, self.rcv2 = refs[3], refs[4]

    def forward(self, piece):
        self.first[piece].wait_recv()
        half = self.half

        def body(cols):
            for k in range(2):
                rows = slice(k * half, (k + 1) * half)
                both = self.own[rows, cols] + self.rcv1[rows, cols]
                self.own[rows, cols] = both
                self.snd2[k][:, cols] = both.astype(jnp.bfloat16)

        tiles(piece, body)
        self.second[piece] = [
            self.links.copy(part(self.snd2[k], piece), part(self.rcv2[1 - k], piece), self.places.to(2))
            for k in range(2)
        ]

    def ready(self, piece):
        for made in self.second[piece]:
            made.wait_recv()

    def value(self, k, cols):
        rows = slice(k * self.half, (k + 1) * self.half)
        return self.own[rows, cols] + self.rcv2[k][:, cols].astype(jnp.float32)


def unit_scratch(rows, width, kind=jnp.float32):
    half, pair = rows // 4, rows // 2
    return [
        pltpu.VMEM((pair, width), kind),
        pltpu.VMEM((pair, width), jnp.float32),
        pltpu.VMEM((pair, width), kind),
        pltpu.VMEM((half, width), jnp.bfloat16),
        pltpu.VMEM((half, width), jnp.bfloat16),
    ]


class Spread:
    def __init__(self, links, ref, places, piece=None, source=None):
        self.links, self.places = links, places
        piece = (0, ref.shape[1]) if piece is None else piece
        mine = part(ref, piece, places.rows[0])
        self.theirs = part(ref, piece, places.rows[2])
        source = mine if source is None else source
        self.out = links.copy(source, mine, places.to(2))
        self.side = links.copy(source, mine, places.to(1))

    def relay(self):
        self.out.wait_recv()
        self.last = self.links.copy(self.theirs, self.theirs, self.places.to(1))

    def finish(self):
        self.side.wait_recv()
        self.last.wait_recv()


class Line:
    def __init__(self, links, ring):
        self.links, self.ring = links, ring
        self.end = ring.me // 2 == ring.me % 2
        self.sent = {True: [], False: []}

    def at_end(self, body):
        pl.when(self.end)(body)

    def at_middle(self, body):
        pl.when(jnp.logical_not(self.end))(body)

    def send(self, end, src, dst, k, land):
        links = self.links
        made = Move(src, dst, links.send, links.recv, links.reserve(1), land, self.ring.to(k))
        made.build().start()
        self.sent[end].append(made)

    def arrive(self, dst, land):
        links = self.links
        Move(dst, dst, links.send, links.recv, land, land, self.ring.to(1)).wait_recv()

    def drain(self):
        @self.at_end
        def _():
            for made in self.sent[True]:
                made.wait_send()

        @self.at_middle
        def _():
            for made in self.sent[False]:
                made.wait_send()


class LineSum:
    def __init__(self, line, source, halves, refs):
        self.line, self.source, self.rows = line, source, line.ring.rows
        self.snd, self.rcv, self.total = refs
        self.lands = {half: line.links.reserve(5) for half in halves}

    def push(self, end, half, k, place, held, to, slot):
        cols = pl.ds(*half)
        value = self.source[self.rows[place], cols]
        if held is not None:
            value = value + self.rcv[held, :, cols].astype(jnp.float32)
        self.snd[k, :, cols] = value.astype(jnp.bfloat16)
        dst = (self.rcv, (slot, slice(None), cols))
        src = (self.snd, (k, slice(None), cols))
        self.line.send(end, src, dst, to, self.lands[half] + slot)

    def arrive(self, half, slot):
        dst = (self.rcv, (slot, slice(None), pl.ds(*half)))
        self.line.arrive(dst, self.lands[half] + slot)

    def start(self, half):
        @self.line.at_end
        def _():
            for k, place in enumerate((3, 2, 1)):
                self.push(True, half, k, place, None, 1, k)

    def hop(self, half, k):
        @self.line.at_middle
        def _():
            self.arrive(half, k)
            self.push(False, half, k, 2 + k, k, 3, 3 + k)

    def turn(self, half):
        @self.line.at_middle
        def _():
            self.arrive(half, 3)
            self.push(False, half, 2, 1, 3, 1, 0)

    def finish(self, half):
        cols = pl.ds(*half)

        def gather(slots):
            value = self.source[self.rows[0], cols]
            for slot in slots:
                self.arrive(half, slot)
                value = value + self.rcv[slot, :, cols].astype(jnp.float32)
            self.total[:, cols] = value

        self.line.at_end(lambda: gather((0,)))
        self.line.at_middle(lambda: gather((2, 4)))
        return self.total[:, cols]


class LineSpread:
    def __init__(self, line, ref, halves, source=None):
        self.line, self.ref, self.source, self.rows = line, ref, source, line.ring.rows
        self.lands = {half: line.links.reserve(3) - 1 for half in halves}

    def spot(self, half, place):
        return part(self.ref, half, self.rows[place])

    def push(self, end, half, place, to, origin):
        dst = self.spot(half, place)
        src = dst if place or self.source is None else part(self.source, half)
        self.line.send(end, src, dst, to, self.lands[half] + origin)

    def arrive(self, half, place):
        self.line.arrive(self.spot(half, place), self.lands[half] + place)

    def start(self, half):
        @self.line.at_end
        def _():
            self.push(True, half, 0, 1, 1)

        @self.line.at_middle
        def _():
            self.push(False, half, 0, 3, 3)
            self.push(False, half, 0, 1, 1)

    def hop(self, half):
        @self.line.at_middle
        def _():
            self.arrive(half, 1)
            self.push(False, half, 1, 3, 2)
            self.arrive(half, 3)
            self.push(False, half, 3, 1, 2)

    def last(self, half):
        @self.line.at_middle
        def _():
            self.arrive(half, 2)
            self.push(False, half, 2, 1, 3)

    def finish(self, half):
        @self.line.at_end
        def _():
            for place in (1, 2, 3):
                self.arrive(half, place)


def arrange(dst, src, places):
    me, sib, far, diag = places.rows
    count = places.count
    for i, rows in enumerate((diag, sib, far, me)):
        dst[i * count : (i + 1) * count, :] = src[rows, :]


def row_scale(scale, lengths):
    position = lax.broadcasted_iota(jnp.int32, scale.shape, 0)
    seq_ids = position // LEN
    within = position - seq_ids * LEN
    limit, counted = jnp.zeros(scale.shape, jnp.int32), 0
    for i in range(lengths.shape[0]):
        length = lengths[i]
        limit = jnp.where(seq_ids == i, length, limit)
        counted = counted + length
    whole = jnp.full(scale.shape, counted, jnp.int32).astype(jnp.float32)
    scale[...] = jnp.where(within < limit, 2.0 / whole, 0.0)


def layer_kernel(flips, *refs):
    refs = iter(refs)

    def take(n):
        return [next(refs) for _ in range(n)]

    (tok, lengths), weights, downs = take(2), take(6), take(3)
    kept_out, loss = take(9), take(1)[0]
    gathered, xp, xq = take(3)
    hidden, grads, cots = take(3), take(4), take(2)
    near, away = take(4), take(4)
    target, diff, scale, part_sums, marked = take(5)
    unit_refs = [take(5) for _ in range(6)]
    ring_refs = [take(3) for _ in range(2)]
    send, recv, wsem, dsem, osem = take(5)

    links, loads, stores = Links(send, recv), Links(None, wsem), Links(None, osem)
    places, ring = Places("split", tok.shape[0]), Places("mp", tok.shape[0])
    mine, turn = places.rows[0], ring.rows[0]
    units = [Unit(links, places, r) for r in unit_refs]
    line = Line(links, ring)
    halves = cuts(target.shape[1], (1, 1))
    rings = [LineSum(line, r, halves, refs) for r, refs in zip((diff, target), ring_refs)]
    turns = [LineSpread(line, cot, halves) for cot in cots]
    moves = LineSpread(line, gathered, halves, tok)
    layers = ((2, (1, 2, 3, 3)), (0, (1,)), (1, (6, 5)))
    pieces = {layer: cuts(units[2 * layer].width, n) for layer, n in layers}
    out = []

    def project(*wbuf):
        waits = {}
        for layer, _ in layers:
            for piece in pieces[layer]:
                for i in (2 * layer, 2 * layer + 1):
                    src, dst = weights[i], wbuf[i]
                    if piece != (0, units[i].width):
                        at = (pl.ds(*piece), slice(None))
                        at = at if flips[i] else at[::-1]
                        src, dst = (src, at), (dst, at)
                    waits[i, piece] = loads.copy(src, dst)
        row_scale(scale, lengths)
        greet([spot.to(k) for spot in (places, ring) for k in (1, 2, 3)])
        for half in halves:
            moves.start(half)
        gathered[turn, :] = tok[...]
        for step in (moves.hop, moves.last, moves.finish):
            for half in halves:
                step(half)
        out.append(stores.copy(gathered, kept_out[0]))
        arrange(xp, gathered, places)
        behind = None
        for layer, _ in layers:
            for piece in pieces[layer]:
                for i in (2 * layer, 2 * layer + 1):
                    waits[i, piece].wait()
                    units[i].multiply(xp, wbuf[i], flips[i], piece)
                    if behind is not None:
                        units[behind[0]].forward(behind[1])
                    behind = (i, piece) if layer != 1 else None

    pl.run_scoped(project, *[pltpu.VMEM(w.shape, jnp.bfloat16) for w in weights])

    def rest(*dbuf):
        waits = {}
        drops = Links(None, dsem)
        for layer, _ in layers:
            for piece in pieces[layer]:
                rows = pl.ds(*piece)
                src, dst = (downs[layer], rows), (dbuf[layer], rows)
                waits[layer, piece] = drops.copy(src, dst)
        spreads = {}

        def activate(layer, piece):
            gate, up = units[2 * layer], units[2 * layer + 1]
            gate.ready(piece)
            up.ready(piece)

            def body(cols):
                g, u = gate.value(cols), up.value(cols)
                sig = jax.nn.sigmoid(g)
                slope = g * sig
                hidden[layer][mine, cols] = (slope * u).astype(jnp.bfloat16)
                if layer < 2:
                    bend = u * sig * (1.0 + g * (1.0 - sig))
                    gate.own[gate.half :, cols] = bend
                    up.own[up.half :, cols] = slope
                    near[2 * layer][:, cols] = bend.astype(jnp.bfloat16)
                    near[2 * layer + 1][:, cols] = slope.astype(jnp.bfloat16)

            tiles(piece, body)
            spreads[layer, piece] = Spread(links, hidden[layer], places, piece)

        wide = (0, target.shape[1])

        def project_down(layer, piece, first, dst, sign):
            spreads[layer, piece].finish()
            waits[layer, piece].wait()
            rows = pl.ds(*piece)

            def body(cols):
                out = jnp.dot(
                    hidden[layer][:, rows],
                    dbuf[layer][rows, cols],
                    preferred_element_type=jnp.float32,
                )
                if first is None:
                    dst[:, cols] += out
                elif sign:
                    dst[:, cols] = out
                else:
                    dst[:, cols] = out - first[:, cols]

            tiles(wide, body, 256)

        for piece in pieces[2]:
            activate(2, piece)
        for piece in pieces[0]:
            activate(0, piece)
        for piece in pieces[1]:
            for i in (2, 3):
                units[i].forward(piece)
        for piece in pieces[2]:
            spreads[2, piece].relay()
        for n, piece in enumerate(pieces[2]):
            project_down(2, piece, None if n else target, target, n == 0)
        for piece in pieces[0]:
            spreads[0, piece].relay()
        for n, piece in enumerate(pieces[0]):
            project_down(0, piece, None if n else target, diff, False)
        out.append(stores.copy(hidden[0], kept_out[1]))
        for half in halves:
            rings[0].start(half)
        for piece in pieces[1]:
            activate(1, piece)
        lent = [links.copy(near[i], away[i], places.to(2)) for i in range(4)]
        for half in halves:
            rings[0].hop(half, 0)
        for n, piece in enumerate(pieces[1]):
            spreads[1, piece].relay()
            if n == 0:
                for half in halves:
                    rings[0].hop(half, 1)
        for half in halves:
            rings[0].turn(half)
        for n, piece in enumerate(pieces[1]):
            project_down(1, piece, None if n else target, target, False)
        out.append(stores.copy(hidden[1], kept_out[2]))
        for half in halves:
            rings[1].start(half)

        factor = scale[turn, 0:1]
        sums = []

        def cotangent(i):
            total_sum = 0.0
            for half in halves:
                total = rings[i].finish(half)
                scaled = factor * total
                cots[i][turn, pl.ds(*half)] = scaled.astype(jnp.bfloat16)
                turns[i].start(half)
                total_sum = total_sum + jnp.sum(scaled * total, keepdims=True)
            sums.append(0.5 * total_sum)

        back, parcels = [], [[], []]
        for i in range(2):
            gate, up = units[2 * i], units[2 * i + 1]
            pair = ((up.snd2, gate.snd2), (up.rcv2, gate.rcv2))
            back.append(Exchange(links, places, (gate.snd1, up.snd1, gate.rcv1, *pair)))
            gate.settle()
            up.settle()

        def differentiate(i, piece):
            back[i].ready(piece)
            half = back[i].half

            def body(cols):
                for k, rows in enumerate((places.rows[2], mine)):
                    value = back[i].value(k, cols)
                    for j in range(2):
                        factor = units[2 * i + j].own[half:, cols] if k else away[2 * i + j][:, cols]
                        out = value * factor.astype(jnp.float32)
                        grads[2 * i + j][rows, cols] = out.astype(jnp.bfloat16)

            tiles(piece, body)
            for j in range(2):
                for rows in (places.rows[2], mine):
                    spot = part(grads[2 * i + j], piece, rows)
                    parcels[i].append(links.copy(spot, spot, places.to(1)))

        def collect(i):
            for made in parcels[i]:
                made.wait_recv()
            for j in range(2):
                out.append(stores.copy(grads[2 * i + j], kept_out[5 + 2 * i + j]))

        def back_project(i, left):
            for half in halves:
                turns[i].finish(half)
            out.append(stores.copy(cots[i], kept_out[3 + i]))
            arrange(left, cots[i], places)
            for piece in pieces[i]:
                back[i].multiply(left, dbuf[i], True, piece)

        cotangent(0)
        for half in halves:
            rings[1].hop(half, 0)
        for half in halves:
            turns[0].hop(half)
        for half in halves:
            rings[1].hop(half, 1)
        for half in halves:
            rings[1].turn(half)
        for half in halves:
            turns[0].last(half)
        cotangent(1)
        row = lax.broadcasted_iota(jnp.int32, part_sums.shape[1:], 0)
        part_sums[0] = jnp.where(row == 0, sums[0], sums[1])
        parts = [
            links.copy((part_sums, 0), (part_sums, k), ring.to(k)) for k in (1, 2, 3)
        ]
        back_project(0, xp)
        for half in halves:
            turns[1].hop(half)
        for piece in pieces[0]:
            back[0].forward(piece)
        for half in halves:
            turns[1].last(half)
        back_project(1, xq)
        for piece in pieces[1]:
            back[1].forward(piece)
        for made in lent:
            made.wait_recv()
        for piece in pieces[0]:
            differentiate(0, piece)
        for move in parts:
            move.wait_recv()
        marked[0] = part_sums[0] + part_sums[1] + part_sums[2] + part_sums[3]
        marks = [
            links.copy((marked, 0), (marked, k), places.to(k)) for k in (1, 2, 3)
        ]
        collect(0)
        for piece in pieces[1]:
            differentiate(1, piece)
        for mark in marks:
            mark.wait_recv()
        loss[...] = marked[0] + marked[1] + marked[2] + marked[3]
        collect(1)
        for made in out:
            made.wait()
        links.drain()
        line.drain()

    pl.run_scoped(rest, *[pltpu.VMEM(d.shape, jnp.bfloat16) for d in downs])


def layer_call(mp, tokens, lengths, weights, downs, flips):
    block, depth = tokens.shape
    rows = block * mp
    widths = [d.shape[0] for d in downs]
    shape, bf16, f32 = jax.ShapeDtypeStruct, jnp.bfloat16, jnp.float32
    outs = [shape((rows, depth), bf16)]
    outs += [shape((rows, widths[i]), bf16) for i in range(2)]
    outs += [shape((rows, depth), bf16)] * 2
    outs += [shape((rows, widths[i // 2]), bf16) for i in range(4)]
    outs.append(shape((8, 128), f32))
    scratch = [pltpu.VMEM((rows, depth), bf16)] * 3
    scratch += [pltpu.VMEM((rows, w), bf16) for w in widths]
    scratch += [pltpu.VMEM((rows, widths[i // 2]), bf16) for i in range(4)]
    scratch += [pltpu.VMEM((rows, depth), bf16)] * 2
    scratch += [pltpu.VMEM((block, widths[i // 2]), bf16) for i in range(4)] * 2
    scratch += [pltpu.VMEM((rows, depth), f32)] * 2
    scratch += [pltpu.VMEM((rows, 128), f32)]
    scratch += [pltpu.VMEM((4, 8, 128), f32)] * 2
    for i in range(6):
        scratch += unit_scratch(rows, widths[i // 2])
    for _ in range(2):
        scratch += [pltpu.VMEM((n, block, depth), bf16) for n in (3, 5)]
        scratch += [pltpu.VMEM((block, depth), f32)]
    copies = 220
    scratch += [pltpu.SemaphoreType.DMA((copies,))] * 2
    scratch += [pltpu.SemaphoreType.DMA((16,))] * 3
    return pl.pallas_call(
        functools.partial(layer_kernel, flips),
        out_shape=outs,
        in_specs=[VMEM, pl.BlockSpec(memory_space=pltpu.SMEM)] + [ANY] * 9,
        out_specs=[ANY] * 9 + [VMEM],
        scratch_shapes=scratch,
        compiler_params=pltpu.CompilerParams(
            collective_id=0, has_side_effects=True, vmem_limit_bytes=GRANT
        ),
    )(tokens, lengths, *weights, *downs)


def gradient_kernel(jobs, *refs):
    refs = iter(refs)

    def take(n):
        return [next(refs) for _ in range(n)]

    sources, loss, outs, losses = take(9), take(1)[0], take(len(jobs)), take(1)[0]
    held, made = take(9), take(len(jobs))
    isem, osem = take(2)
    order = list(dict.fromkeys(i for job in jobs for i in job))
    loads = {i: pltpu.make_async_copy(sources[i], held[i], isem.at[i]) for i in order}
    for i in order:
        loads[i].start()
    for i in range(losses.shape[0]):
        losses[i] = loss[i, 0]
    for j, job in enumerate(jobs):
        for i in job:
            if i in loads:
                loads.pop(i).wait()
        left, right, dst = held[job[0]], held[job[1]], made[j]
        height, width = dst.shape
        step = -(-height // 256) * 128
        for start in range(0, height, step):
            rows = pl.ds(start, min(step, height - start))
            for at in range(0, width, 256):
                cols = pl.ds(at, min(256, width - at))
                dst[rows, cols] = contract_rows(left[:, rows], right[:, cols]).astype(dst.dtype)
            pltpu.make_async_copy(dst.at[rows], outs[j].at[rows], osem.at[j]).start()
    for j in range(len(jobs)):
        pltpu.make_async_copy(made[j], outs[j], osem.at[j]).wait()


def gradient_call(arrays, loss, jobs, students):
    shape = jax.ShapeDtypeStruct
    outs = [shape((arrays[a].shape[1], arrays[b].shape[1]), jnp.bfloat16) for a, b in jobs]
    smem = pl.BlockSpec(memory_space=pltpu.SMEM)
    scratch = [pltpu.VMEM(item.shape, item.dtype) for item in (*arrays, *outs)]
    scratch += [pltpu.SemaphoreType.DMA((len(arrays),)), pltpu.SemaphoreType.DMA((len(jobs),))]
    return pl.pallas_call(
        functools.partial(gradient_kernel, jobs),
        out_shape=outs + [shape((students,), jnp.float32)],
        in_specs=[ANY] * len(arrays) + [smem],
        out_specs=[ANY] * len(jobs) + [smem],
        scratch_shapes=scratch,
        compiler_params=pltpu.CompilerParams(vmem_limit_bytes=GRANT),
    )(*arrays, loss)


def per_device_kernels(
    mp,
    tokens,
    lengths,
    teacher_gate,
    teacher_up,
    teacher_down,
    first_gate,
    first_up,
    first_down,
    second_gate,
    second_up,
    second_down,
):
    weights, flips = [], []
    for w in (first_gate, first_up, second_gate, second_up, teacher_gate, teacher_up):
        flip = w.shape[1] % 128 != 0
        flips.append(flip)
        weights.append(w.T if flip else w)
    *arrays, loss = layer_call(
        mp, tokens, lengths, weights, (first_down, second_down, teacher_down), tuple(flips)
    )
    jobs = [(1, 3), (2, 4)]
    jobs += [(5 + i, 0) if flips[i] else (0, 5 + i) for i in range(4)]
    made = gradient_call(arrays, loss, tuple(jobs), 2)
    ins = [out.T if flip else out for out, flip in zip(made[2:6], flips)]
    return ins[0], ins[1], made[0], ins[2], ins[3], made[1], made[6]


def per_device(
    tokens,
    lengths,
    teacher_gate,
    teacher_up,
    teacher_down,
    first_gate,
    first_up,
    first_down,
    second_gate,
    second_up,
    second_down,
):
    gathered = lax.all_gather(tokens, "mp", axis=0, tiled=True)
    total_rows = gathered.shape[0]

    def project(weight):
        return jnp.dot(gathered, weight, preferred_element_type=jnp.float32)

    partials = (
        project(teacher_gate),
        project(teacher_up),
        project(first_gate),
        project(first_up),
        project(second_gate),
        project(second_up),
    )
    values = lax.psum(
        (partials[0], partials[1], partials[2], partials[3], partials[4], partials[5]), "split"
    )
    hidden = (
        activate(values[0], values[1]),
        activate(values[2], values[3]),
        activate(values[4], values[5]),
    )
    target = jnp.dot(hidden[0], teacher_down, preferred_element_type=jnp.float32)
    diffs = (
        jnp.dot(hidden[1], first_down, preferred_element_type=jnp.float32) - target,
        jnp.dot(hidden[2], second_down, preferred_element_type=jnp.float32) - target,
    )
    counted = jnp.sum(lengths).astype(jnp.float32)
    summed = lax.psum((diffs[0], diffs[1]), "mp")
    mask = valid_rows(lengths, total_rows)
    partial_loss = (
        jnp.stack([jnp.sum(mask * summed[0] * summed[0]), jnp.sum(mask * summed[1] * summed[1])])
        / counted
    )
    losses = lax.psum(partial_loss, "split")
    cotangents = (
        (2.0 * mask * summed[0] / counted).astype(jnp.bfloat16),
        (2.0 * mask * summed[1] / counted).astype(jnp.bfloat16),
    )
    grad_first_down = contract_rows(hidden[1], cotangents[0]).astype(jnp.bfloat16)
    grad_second_down = contract_rows(hidden[2], cotangents[1]).astype(jnp.bfloat16)
    dims = (((1,), (1,)), ((), ()))
    backs = (
        lax.dot_general(cotangents[0], first_down, dims, preferred_element_type=jnp.float32),
        lax.dot_general(cotangents[1], second_down, dims, preferred_element_type=jnp.float32),
    )
    back_full = lax.psum((backs[0], backs[1]), "split")
    first_dg, first_du = hidden_grads(back_full[0], values[2], values[3])
    second_dg, second_du = hidden_grads(back_full[1], values[4], values[5])
    grads_in = (first_dg, first_du, second_dg, second_du)
    outputs = tuple((contract_rows(gathered, item).astype(jnp.bfloat16) for item in grads_in))
    return (
        outputs[0],
        outputs[1],
        grad_first_down,
        outputs[2],
        outputs[3],
        grad_second_down,
        losses,
    )


def run(mp, split, *args):
    rows = args[0].shape[0] * mp
    if split == 4 and mp == 4 and args[0].shape[0] % 16 == 0 and rows % 64 == 0:
        return per_device_kernels(mp, *args)
    return per_device(*args)


def solution(mesh):
    placed = (
        P(("parts", "mp"), "split"),
        P("parts"),
        P(("parts", "split"), "mp"),
        P(("parts", "split"), "mp"),
        P(("parts", "mp"), "split"),
        P(("parts", "split"), "mp"),
        P(("parts", "split"), "mp"),
        P(("parts", "mp"), "split"),
        P(("parts", "split"), "mp"),
        P(("parts", "split"), "mp"),
        P(("parts", "mp"), "split"),
    )
    return jax.shard_map(
        functools.partial(run, mesh.shape["mp"], mesh.shape["split"]),
        mesh=mesh,
        in_specs=placed,
        out_specs=(
            P(("parts", "split"), "mp"),
            P(("parts", "split"), "mp"),
            P(("parts", "mp"), "split"),
            P(("parts", "split"), "mp"),
            P(("parts", "split"), "mp"),
            P(("parts", "mp"), "split"),
            P("parts"),
        ),
        check_vma=False,
    )
```

```python
import functools

import jax
import jax.numpy as jnp
from jax import lax
from jax.experimental import pallas as pl
from jax.experimental.pallas import tpu as pltpu
from jax.sharding import PartitionSpec as P

MESH = pl.DeviceIdType.MESH
VMEM = pl.BlockSpec(memory_space=pltpu.VMEM)
ANY = pl.BlockSpec(memory_space=pl.ANY)
TILE = 384
GRANT = 67043328

LEN = 64


def contract_rows(left, right):
    return lax.dot_general(
        left, right, (((0,), (0,)), ((), ())), preferred_element_type=jnp.float32
    )


def valid_rows(lengths, count):
    position = jnp.arange(count, dtype=jnp.int32)
    seq_ids = position // LEN
    within = position - seq_ids * LEN
    limit = jnp.sum(
        jnp.where(
            seq_ids[:, None] == jnp.arange(lengths.shape[0], dtype=jnp.int32)[None, :],
            lengths[None, :],
            0,
        ),
        axis=1,
    )
    return (within < limit).astype(jnp.float32)[:, None]


def activate(gate, up):
    return (jax.nn.silu(gate) * up).astype(jnp.bfloat16)


def hidden_grads(back, gate, up):
    sig = jax.nn.sigmoid(gate)
    dgate = (back * up * sig * (1.0 + gate * (1.0 - sig))).astype(jnp.bfloat16)
    dup = (back * gate * sig).astype(jnp.bfloat16)
    return (dgate, dup)


def view(spot):
    return spot[0].at[spot[1]] if isinstance(spot, tuple) else spot


class Move:
    def __init__(self, *args):
        self.args = args

    def build(self):
        src, dst, send, recv, at, land, device = self.args
        if device is None:
            return pltpu.make_async_copy(view(src), view(dst), recv.at[land])
        return pltpu.make_async_remote_copy(
            src_ref=view(src),
            dst_ref=view(dst),
            send_sem=send.at[at],
            recv_sem=recv.at[land],
            device_id=device,
            device_id_type=MESH,
        )

    def wait(self):
        self.build().wait()

    def wait_recv(self):
        self.build().wait_recv()

    def wait_send(self):
        self.build().wait_send()


class Links:
    def __init__(self, send, recv):
        self.send, self.recv, self.count, self.made = send, recv, 0, []

    def copy(self, src, dst, device=None):
        at = self.reserve(1)
        made = Move(src, dst, self.send, self.recv, at, at, device)
        made.build().start()
        self.made.append(made)
        return made

    def reserve(self, count):
        at = self.count
        self.count += count
        return at

    def settle(self, made):
        made.wait_send()
        self.made.remove(made)

    def drain(self):
        for made in self.made:
            made.wait_send()


def greet(devices):
    barrier = pltpu.get_barrier_semaphore()
    for device in devices:
        pl.semaphore_signal(barrier, inc=1, device_id=device, device_id_type=MESH)
    pl.semaphore_wait(barrier, len(devices))


def cuts(width, shares):
    if width % 128:
        return [(0, width)]
    lanes, whole, made, taken, start = width // 128, sum(shares), [], 0, 0
    for share in shares:
        taken += share
        end = lanes * taken // whole * 128
        if end > start:
            made.append((start, end - start))
        start = end
    return made


def tiles(piece, body, tile=TILE):
    start, width = piece
    full = width // tile
    if full == 1:
        body(pl.ds(start, tile))
    elif full:

        @pl.loop(0, full)
        def _(i):
            body(pl.ds(pl.multiple_of(start + i * tile, 128), tile))

    if width % tile:
        body(pl.ds(start + full * tile, width % tile))


def four_places(axis):
    me = lax.axis_index(axis)
    chip, core = me // 2, me % 2
    sib = chip * 2 + (1 - core)
    far = (1 - chip) * 2 + core
    diag = (1 - chip) * 2 + (1 - core)
    return me, sib, far, diag


class Places:
    def __init__(self, axis, count):
        self.axis, self.count = axis, count
        self.me, self.sib, self.far, self.diag = self.ids = four_places(axis)
        self.rows = [rows_at(place, count) for place in self.ids]

    def to(self, k):
        return {self.axis: self.ids[k]}


def rows_at(block, count):
    return pl.ds(pl.multiple_of(block * count, 16), count)


def part(ref, piece, rows=slice(None)):
    return ref, (rows, pl.ds(*piece))


class Unit:
    def __init__(self, links, places, refs):
        self.links, self.places = links, places
        self.snd1, self.own, self.rcv1, self.snd2, self.rcv2 = refs
        self.half = self.own.shape[0] // 2
        self.width = self.own.shape[1]
        self.first, self.second = {}, {}

    def pass_on(self, piece):
        self.first[piece] = self.links.copy(
            part(self.snd1, piece), part(self.rcv1, piece), self.places.to(1)
        )

    def multiply(self, left, weight, flip, piece):
        pair = 2 * self.half

        def body(cols):
            if flip:
                right, dims = weight[cols, :], (((1,), (1,)), ((), ()))
            else:
                right, dims = weight[:, cols], (((1,), (0,)), ((), ()))
            out = lax.dot_general(left[...], right, dims, preferred_element_type=jnp.float32)
            self.snd1[:, cols] = out[:pair].astype(self.snd1.dtype)
            self.own[:, cols] = out[pair:]

        tiles(piece, body)
        self.pass_on(piece)

    def forward(self, piece):
        self.first[piece].wait_recv()
        half = self.half

        def body(cols):
            both = self.own[:half, cols] + self.rcv1[:half, cols].astype(jnp.float32)
            self.snd2[:, cols] = both.astype(jnp.bfloat16)

        tiles(piece, body)
        self.second[piece] = self.links.copy(
            part(self.snd2, piece), part(self.rcv2, piece), self.places.to(2)
        )

    def ready(self, piece):
        self.second[piece].wait_recv()

    def value(self, cols):
        half = self.half
        return (
            self.own[half:, cols]
            + self.rcv1[half:, cols].astype(jnp.float32)
            + self.rcv2[:, cols].astype(jnp.float32)
        )

    def settle(self):
        for made in (*self.first.values(), *self.second.values()):
            self.links.settle(made)


class Exchange(Unit):
    def __init__(self, links, places, refs):
        super().__init__(links, places, (*refs[:3], None, None))
        self.snd2, self.rcv2 = refs[3], refs[4]

    def forward(self, piece):
        self.first[piece].wait_recv()
        half = self.half

        def body(cols):
            for k in range(2):
                rows = slice(k * half, (k + 1) * half)
                both = self.own[rows, cols] + self.rcv1[rows, cols]
                self.own[rows, cols] = both
                self.snd2[k][:, cols] = both.astype(jnp.bfloat16)

        tiles(piece, body)
        self.second[piece] = [
            self.links.copy(part(self.snd2[k], piece), part(self.rcv2[1 - k], piece), self.places.to(2))
            for k in range(2)
        ]

    def ready(self, piece):
        for made in self.second[piece]:
            made.wait_recv()

    def value(self, k, cols):
        rows = slice(k * self.half, (k + 1) * self.half)
        return self.own[rows, cols] + self.rcv2[k][:, cols].astype(jnp.float32)


def unit_scratch(rows, width, kind=jnp.float32):
    half, pair = rows // 4, rows // 2
    return [
        pltpu.VMEM((pair, width), kind),
        pltpu.VMEM((pair, width), jnp.float32),
        pltpu.VMEM((pair, width), kind),
        pltpu.VMEM((half, width), jnp.bfloat16),
        pltpu.VMEM((half, width), jnp.bfloat16),
    ]


class Spread:
    def __init__(self, links, ref, places, piece=None, source=None):
        self.links, self.places = links, places
        piece = (0, ref.shape[1]) if piece is None else piece
        mine = part(ref, piece, places.rows[0])
        self.theirs = part(ref, piece, places.rows[2])
        source = mine if source is None else part(source, piece)
        self.out = links.copy(source, mine, places.to(2))
        self.side = links.copy(source, mine, places.to(1))

    def relay(self):
        self.out.wait_recv()
        self.last = self.links.copy(self.theirs, self.theirs, self.places.to(1))

    def finish(self):
        self.side.wait_recv()
        self.last.wait_recv()


class Line:
    def __init__(self, links, ring):
        self.links, self.ring = links, ring
        self.end = ring.me // 2 == ring.me % 2
        self.sent = {True: [], False: []}

    def at_end(self, body):
        pl.when(self.end)(body)

    def at_middle(self, body):
        pl.when(jnp.logical_not(self.end))(body)

    def send(self, end, src, dst, k, land):
        links = self.links
        made = Move(src, dst, links.send, links.recv, links.reserve(1), land, self.ring.to(k))
        made.build().start()
        self.sent[end].append(made)

    def arrive(self, dst, land):
        links = self.links
        Move(dst, dst, links.send, links.recv, land, land, self.ring.to(1)).wait_recv()

    def drain(self):
        @self.at_end
        def _():
            for made in self.sent[True]:
                made.wait_send()

        @self.at_middle
        def _():
            for made in self.sent[False]:
                made.wait_send()


class LineSum:
    def __init__(self, line, source, halves, refs):
        self.line, self.source, self.rows = line, source, line.ring.rows
        self.snd, self.rcv, self.total = refs
        self.lands = {half: line.links.reserve(5) for half in halves}

    def push(self, end, half, k, place, held, to, slot):
        cols = pl.ds(*half)
        value = self.source[self.rows[place], cols]
        if held is not None:
            value = value + self.rcv[held, :, cols].astype(jnp.float32)
        self.snd[k, :, cols] = value.astype(jnp.bfloat16)
        dst = (self.rcv, (slot, slice(None), cols))
        src = (self.snd, (k, slice(None), cols))
        self.line.send(end, src, dst, to, self.lands[half] + slot)

    def arrive(self, half, slot):
        dst = (self.rcv, (slot, slice(None), pl.ds(*half)))
        self.line.arrive(dst, self.lands[half] + slot)

    def start(self, half):
        @self.line.at_end
        def _():
            for k, place in enumerate((3, 2, 1)):
                self.push(True, half, k, place, None, 1, k)

    def hop(self, half, k):
        @self.line.at_middle
        def _():
            self.arrive(half, k)
            self.push(False, half, k, 2 + k, k, 3, 3 + k)

    def turn(self, half):
        @self.line.at_middle
        def _():
            self.arrive(half, 3)
            self.push(False, half, 2, 1, 3, 1, 0)

    def finish(self, half):
        cols = pl.ds(*half)

        def gather(slots):
            value = self.source[self.rows[0], cols]
            for slot in slots:
                self.arrive(half, slot)
                value = value + self.rcv[slot, :, cols].astype(jnp.float32)
            self.total[:, cols] = value

        self.line.at_end(lambda: gather((0,)))
        self.line.at_middle(lambda: gather((2, 4)))
        return self.total[:, cols]


class DirectSum:
    def __init__(self, line, source, refs):
        self.links, self.ring, self.source = line.links, line.ring, source
        self.snd, self.rcv = refs[:2]
        self.made = {}

    def start(self, half):
        cols = pl.ds(*half)
        moves = []
        for place in (3, 2, 1):
            spot = (place - 1, slice(None), cols)
            self.snd[spot] = self.source[self.ring.rows[place], cols].astype(jnp.bfloat16)
            moves.append(
                self.links.copy((self.snd, spot), (self.rcv, spot), self.ring.to(place))
            )
        self.made[half] = moves

    def finish(self, half):
        cols = pl.ds(*half)
        value = self.source[self.ring.rows[0], cols]
        for slot, made in zip((2, 1, 0), self.made[half]):
            made.wait_recv()
            value = value + self.rcv[slot, :, cols].astype(jnp.float32)
        return value


class LineSpread:
    def __init__(self, line, ref, halves, source=None):
        self.line, self.ref, self.source, self.rows = line, ref, source, line.ring.rows
        self.lands = {half: line.links.reserve(3) - 1 for half in halves}

    def spot(self, half, place):
        return part(self.ref, half, self.rows[place])

    def push(self, end, half, place, to, origin):
        dst = self.spot(half, place)
        src = dst if place or self.source is None else part(self.source, half)
        self.line.send(end, src, dst, to, self.lands[half] + origin)

    def arrive(self, half, place):
        self.line.arrive(self.spot(half, place), self.lands[half] + place)

    def start(self, half):
        @self.line.at_end
        def _():
            self.push(True, half, 0, 1, 1)

        @self.line.at_middle
        def _():
            self.push(False, half, 0, 3, 3)
            self.push(False, half, 0, 1, 1)

    def hop(self, half):
        @self.line.at_middle
        def _():
            self.arrive(half, 1)
            self.push(False, half, 1, 3, 2)
            self.arrive(half, 3)
            self.push(False, half, 3, 1, 2)

    def last(self, half):
        @self.line.at_middle
        def _():
            self.arrive(half, 2)
            self.push(False, half, 2, 1, 3)

    def finish(self, half):
        @self.line.at_end
        def _():
            for place in (1, 2, 3):
                self.arrive(half, place)


def arrange(dst, src, places):
    me, sib, far, diag = places.rows
    count = places.count
    for i, rows in enumerate((diag, sib, far, me)):
        dst[i * count : (i + 1) * count, :] = src[rows, :]


def row_scale(scale, lengths):
    position = lax.broadcasted_iota(jnp.int32, scale.shape, 0)
    seq_ids = position // LEN
    within = position - seq_ids * LEN
    limit, counted = jnp.zeros(scale.shape, jnp.int32), 0
    for i in range(lengths.shape[0]):
        length = lengths[i]
        limit = jnp.where(seq_ids == i, length, limit)
        counted = counted + length
    whole = jnp.full(scale.shape, counted, jnp.int32).astype(jnp.float32)
    scale[...] = jnp.where(within < limit, 2.0 / whole, 0.0)


def layer_kernel(flips, *refs):
    refs = iter(refs)

    def take(n):
        return [next(refs) for _ in range(n)]

    (tok, lengths), weights, downs = take(2), take(6), take(3)
    kept_out, loss = take(9), take(1)[0]
    gathered, xp, xq = take(3)
    hidden, grads, cots = take(3), take(4), take(2)
    near, away = take(4), take(4)
    target, diff, scale, part_sums, marked = take(5)
    unit_refs = [take(5) for _ in range(6)]
    ring_refs = [take(3) for _ in range(2)]
    send, recv, wsem, dsem, osem = take(5)

    links, loads, stores = Links(send, recv), Links(None, wsem), Links(None, osem)
    places, ring = Places("split", tok.shape[0]), Places("mp", tok.shape[0])
    mine, turn = places.rows[0], ring.rows[0]
    units = [Unit(links, places, r) for r in unit_refs]
    line = Line(links, ring)
    halves, slabs = cuts(target.shape[1], (1, 1)), cuts(target.shape[1], (6, 4))
    rings = [LineSum(line, diff, halves, ring_refs[0]), DirectSum(line, target, ring_refs[1])]
    turns = LineSpread(line, cots[0], halves)
    layers = ((2, (1, 2, 3, 3)), (0, (1,)), (1, (6, 5)))
    pieces = {layer: cuts(units[2 * layer].width, n) for layer, n in layers}
    out = []

    def project(*wbuf):
        waits = {}
        for layer, _ in layers:
            for piece in pieces[layer]:
                for i in (2 * layer, 2 * layer + 1):
                    src, dst = weights[i], wbuf[i]
                    if piece != (0, units[i].width):
                        at = (pl.ds(*piece), slice(None))
                        at = at if flips[i] else at[::-1]
                        src, dst = (src, at), (dst, at)
                    waits[i, piece] = loads.copy(src, dst)
        row_scale(scale, lengths)
        greet([spot.to(k) for spot in (places, ring) for k in (1, 2, 3)])
        moves = [Spread(links, gathered, ring, half, tok) for half in halves]
        gathered[turn, :] = tok[...]
        for move in moves:
            move.relay()
        for move in moves:
            move.finish()
        out.append(stores.copy(gathered, kept_out[0]))
        arrange(xp, gathered, places)
        behind = None
        for layer, _ in layers:
            for piece in pieces[layer]:
                for i in (2 * layer, 2 * layer + 1):
                    waits[i, piece].wait()
                    units[i].multiply(xp, wbuf[i], flips[i], piece)
                    if behind is not None:
                        units[behind[0]].forward(behind[1])
                    behind = (i, piece) if layer != 1 else None

    pl.run_scoped(project, *[pltpu.VMEM(w.shape, jnp.bfloat16) for w in weights])

    def rest(*dbuf):
        waits = {}
        drops = Links(None, dsem)
        for layer, _ in layers:
            for piece in pieces[layer]:
                rows = pl.ds(*piece)
                src, dst = (downs[layer], rows), (dbuf[layer], rows)
                waits[layer, piece] = drops.copy(src, dst)
        spreads = {}

        def activate(layer, piece):
            gate, up = units[2 * layer], units[2 * layer + 1]
            gate.ready(piece)
            up.ready(piece)

            def body(cols):
                g, u = gate.value(cols), up.value(cols)
                sig = jax.nn.sigmoid(g)
                slope = g * sig
                hidden[layer][mine, cols] = (slope * u).astype(jnp.bfloat16)
                if layer < 2:
                    bend = u * sig * (1.0 + g * (1.0 - sig))
                    gate.own[gate.half :, cols] = bend
                    up.own[up.half :, cols] = slope
                    near[2 * layer][:, cols] = bend.astype(jnp.bfloat16)
                    near[2 * layer + 1][:, cols] = slope.astype(jnp.bfloat16)

            tiles(piece, body)
            spreads[layer, piece] = Spread(links, hidden[layer], places, piece)

        wide = (0, target.shape[1])

        def project_down(layer, piece, first, dst, sign):
            spreads[layer, piece].finish()
            waits[layer, piece].wait()
            rows = pl.ds(*piece)

            def body(cols):
                out = jnp.dot(
                    hidden[layer][:, rows],
                    dbuf[layer][rows, cols],
                    preferred_element_type=jnp.float32,
                )
                if first is None:
                    dst[:, cols] += out
                elif sign:
                    dst[:, cols] = out
                else:
                    dst[:, cols] = out - first[:, cols]

            tiles(wide, body, 256)

        for piece in pieces[2]:
            activate(2, piece)
        for piece in pieces[0]:
            activate(0, piece)
        for piece in pieces[1]:
            for i in (2, 3):
                units[i].forward(piece)
        for piece in pieces[2]:
            spreads[2, piece].relay()
        for n, piece in enumerate(pieces[2]):
            project_down(2, piece, None if n else target, target, n == 0)
        for piece in pieces[0]:
            spreads[0, piece].relay()
        for n, piece in enumerate(pieces[0]):
            project_down(0, piece, None if n else target, diff, False)
        out.append(stores.copy(hidden[0], kept_out[1]))
        for half in halves:
            rings[0].start(half)
        for piece in pieces[1]:
            activate(1, piece)
        lent = [links.copy(near[i], away[i], places.to(2)) for i in range(4)]
        for half in halves:
            rings[0].hop(half, 0)
        for n, piece in enumerate(pieces[1]):
            spreads[1, piece].relay()
            if n == 0:
                for half in halves:
                    rings[0].hop(half, 1)
        for half in halves:
            rings[0].turn(half)
        for n, piece in enumerate(pieces[1]):
            project_down(1, piece, None if n else target, target, False)
        out.append(stores.copy(hidden[1], kept_out[2]))
        for slab in slabs:
            rings[1].start(slab)

        factor = scale[turn, 0:1]

        def cotangent(i, half):
            total = rings[i].finish(half)
            scaled = factor * total
            cots[i][turn, pl.ds(*half)] = scaled.astype(jnp.bfloat16)
            return 0.5 * jnp.sum(scaled * total, keepdims=True)

        back, parcels = [], [[], []]
        for i in range(2):
            gate, up = units[2 * i], units[2 * i + 1]
            pair = ((up.snd2, gate.snd2), (up.rcv2, gate.rcv2))
            back.append(Exchange(links, places, (gate.snd1, up.snd1, gate.rcv1, *pair)))
            gate.settle()
            up.settle()

        def differentiate(i, piece):
            back[i].ready(piece)
            half = back[i].half

            def body(cols):
                for k, rows in enumerate((places.rows[2], mine)):
                    value = back[i].value(k, cols)
                    for j in range(2):
                        factor = units[2 * i + j].own[half:, cols] if k else away[2 * i + j][:, cols]
                        out = value * factor.astype(jnp.float32)
                        grads[2 * i + j][rows, cols] = out.astype(jnp.bfloat16)

            tiles(piece, body)
            for j in range(2):
                for rows in (places.rows[2], mine):
                    spot = part(grads[2 * i + j], piece, rows)
                    parcels[i].append(links.copy(spot, spot, places.to(1)))

        def collect(i):
            for made in parcels[i]:
                made.wait_recv()
            for j in range(2):
                out.append(stores.copy(grads[2 * i + j], kept_out[5 + 2 * i + j]))

        def back_project(i, left):
            out.append(stores.copy(cots[i], kept_out[3 + i]))
            arrange(left, cots[i], places)
            for piece in pieces[i]:
                back[i].multiply(left, dbuf[i], True, piece)

        sums, relays = [0.0, 0.0], []
        for half in halves:
            sums[0] = sums[0] + cotangent(0, half)
            turns.start(half)
        for half in halves:
            turns.hop(half)
        for n, slab in enumerate(slabs):
            sums[1] = sums[1] + cotangent(1, slab)
            relays.append(Spread(links, cots[1], ring, slab))
            if n == 0:
                for half in halves:
                    turns.last(half)
        row = lax.broadcasted_iota(jnp.int32, part_sums.shape[1:], 0)
        part_sums[0] = jnp.where(row == 0, sums[0], sums[1])
        parts = [
            links.copy((part_sums, 0), (part_sums, k), ring.to(k)) for k in (1, 2, 3)
        ]
        relays[0].relay()
        for half in halves:
            turns.finish(half)
        back_project(0, xp)
        for relay in relays[1:]:
            relay.relay()
        for piece in pieces[0]:
            back[0].forward(piece)
        for relay in relays:
            relay.finish()
        back_project(1, xq)
        for piece in pieces[1]:
            back[1].forward(piece)
        for made in lent:
            made.wait_recv()
        for piece in pieces[0]:
            differentiate(0, piece)
        for move in parts:
            move.wait_recv()
        marked[0] = part_sums[0] + part_sums[1] + part_sums[2] + part_sums[3]
        marks = [
            links.copy((marked, 0), (marked, k), places.to(k)) for k in (1, 2, 3)
        ]
        collect(0)
        for piece in pieces[1]:
            differentiate(1, piece)
        for mark in marks:
            mark.wait_recv()
        loss[...] = marked[0] + marked[1] + marked[2] + marked[3]
        collect(1)
        for made in out:
            made.wait()
        links.drain()
        line.drain()

    pl.run_scoped(rest, *[pltpu.VMEM(d.shape, jnp.bfloat16) for d in downs])


def layer_call(mp, tokens, lengths, weights, downs, flips):
    block, depth = tokens.shape
    rows = block * mp
    widths = [d.shape[0] for d in downs]
    shape, bf16, f32 = jax.ShapeDtypeStruct, jnp.bfloat16, jnp.float32
    outs = [shape((rows, depth), bf16)]
    outs += [shape((rows, widths[i]), bf16) for i in range(2)]
    outs += [shape((rows, depth), bf16)] * 2
    outs += [shape((rows, widths[i // 2]), bf16) for i in range(4)]
    outs.append(shape((8, 128), f32))
    scratch = [pltpu.VMEM((rows, depth), bf16)] * 3
    scratch += [pltpu.VMEM((rows, w), bf16) for w in widths]
    scratch += [pltpu.VMEM((rows, widths[i // 2]), bf16) for i in range(4)]
    scratch += [pltpu.VMEM((rows, depth), bf16)] * 2
    scratch += [pltpu.VMEM((block, widths[i // 2]), bf16) for i in range(4)] * 2
    scratch += [pltpu.VMEM((rows, depth), f32)] * 2
    scratch += [pltpu.VMEM((rows, 128), f32)]
    scratch += [pltpu.VMEM((4, 8, 128), f32)] * 2
    for i in range(6):
        scratch += unit_scratch(rows, widths[i // 2])
    for _ in range(2):
        scratch += [pltpu.VMEM((n, block, depth), bf16) for n in (3, 5)]
        scratch += [pltpu.VMEM((block, depth), f32)]
    copies = 220
    scratch += [pltpu.SemaphoreType.DMA((copies,))] * 2
    scratch += [pltpu.SemaphoreType.DMA((16,))] * 3
    return pl.pallas_call(
        functools.partial(layer_kernel, flips),
        out_shape=outs,
        in_specs=[VMEM, pl.BlockSpec(memory_space=pltpu.SMEM)] + [ANY] * 9,
        out_specs=[ANY] * 9 + [VMEM],
        scratch_shapes=scratch,
        compiler_params=pltpu.CompilerParams(
            collective_id=0, has_side_effects=True, vmem_limit_bytes=GRANT
        ),
    )(tokens, lengths, *weights, *downs)


def gradient_kernel(jobs, *refs):
    refs = iter(refs)

    def take(n):
        return [next(refs) for _ in range(n)]

    sources, loss, outs, losses = take(9), take(1)[0], take(len(jobs)), take(1)[0]
    held, made = take(9), take(len(jobs))
    isem, osem = take(2)
    order = list(dict.fromkeys(i for job in jobs for i in job))
    loads = {i: pltpu.make_async_copy(sources[i], held[i], isem.at[i]) for i in order}
    for i in order:
        loads[i].start()
    for i in range(losses.shape[0]):
        losses[i] = loss[i, 0]
    for j, job in enumerate(jobs):
        for i in job:
            if i in loads:
                loads.pop(i).wait()
        left, right, dst = held[job[0]], held[job[1]], made[j]
        height, width = dst.shape
        step = -(-height // 256) * 128
        for start in range(0, height, step):
            rows = pl.ds(start, min(step, height - start))
            for at in range(0, width, 256):
                cols = pl.ds(at, min(256, width - at))
                dst[rows, cols] = contract_rows(left[:, rows], right[:, cols]).astype(dst.dtype)
            pltpu.make_async_copy(dst.at[rows], outs[j].at[rows], osem.at[j]).start()
    for j in range(len(jobs)):
        pltpu.make_async_copy(made[j], outs[j], osem.at[j]).wait()


def gradient_call(arrays, loss, jobs, students):
    shape = jax.ShapeDtypeStruct
    outs = [shape((arrays[a].shape[1], arrays[b].shape[1]), jnp.bfloat16) for a, b in jobs]
    smem = pl.BlockSpec(memory_space=pltpu.SMEM)
    scratch = [pltpu.VMEM(item.shape, item.dtype) for item in (*arrays, *outs)]
    scratch += [pltpu.SemaphoreType.DMA((len(arrays),)), pltpu.SemaphoreType.DMA((len(jobs),))]
    return pl.pallas_call(
        functools.partial(gradient_kernel, jobs),
        out_shape=outs + [shape((students,), jnp.float32)],
        in_specs=[ANY] * len(arrays) + [smem],
        out_specs=[ANY] * len(jobs) + [smem],
        scratch_shapes=scratch,
        compiler_params=pltpu.CompilerParams(vmem_limit_bytes=GRANT),
    )(*arrays, loss)


def per_device_kernels(
    mp,
    tokens,
    lengths,
    teacher_gate,
    teacher_up,
    teacher_down,
    first_gate,
    first_up,
    first_down,
    second_gate,
    second_up,
    second_down,
):
    weights, flips = [], []
    for w in (first_gate, first_up, second_gate, second_up, teacher_gate, teacher_up):
        flip = w.shape[1] % 128 != 0
        flips.append(flip)
        weights.append(w.T if flip else w)
    *arrays, loss = layer_call(
        mp, tokens, lengths, weights, (first_down, second_down, teacher_down), tuple(flips)
    )
    jobs = [(1, 3), (2, 4)]
    jobs += [(5 + i, 0) if flips[i] else (0, 5 + i) for i in range(4)]
    made = gradient_call(arrays, loss, tuple(jobs), 2)
    ins = [out.T if flip else out for out, flip in zip(made[2:6], flips)]
    return ins[0], ins[1], made[0], ins[2], ins[3], made[1], made[6]


def per_device(
    tokens,
    lengths,
    teacher_gate,
    teacher_up,
    teacher_down,
    first_gate,
    first_up,
    first_down,
    second_gate,
    second_up,
    second_down,
):
    gathered = lax.all_gather(tokens, "mp", axis=0, tiled=True)
    total_rows = gathered.shape[0]

    def project(weight):
        return jnp.dot(gathered, weight, preferred_element_type=jnp.float32)

    partials = (
        project(teacher_gate),
        project(teacher_up),
        project(first_gate),
        project(first_up),
        project(second_gate),
        project(second_up),
    )
    values = lax.psum(
        (partials[0], partials[1], partials[2], partials[3], partials[4], partials[5]), "split"
    )
    hidden = (
        activate(values[0], values[1]),
        activate(values[2], values[3]),
        activate(values[4], values[5]),
    )
    target = jnp.dot(hidden[0], teacher_down, preferred_element_type=jnp.float32)
    diffs = (
        jnp.dot(hidden[1], first_down, preferred_element_type=jnp.float32) - target,
        jnp.dot(hidden[2], second_down, preferred_element_type=jnp.float32) - target,
    )
    counted = jnp.sum(lengths).astype(jnp.float32)
    summed = lax.psum((diffs[0], diffs[1]), "mp")
    mask = valid_rows(lengths, total_rows)
    partial_loss = (
        jnp.stack([jnp.sum(mask * summed[0] * summed[0]), jnp.sum(mask * summed[1] * summed[1])])
        / counted
    )
    losses = lax.psum(partial_loss, "split")
    cotangents = (
        (2.0 * mask * summed[0] / counted).astype(jnp.bfloat16),
        (2.0 * mask * summed[1] / counted).astype(jnp.bfloat16),
    )
    grad_first_down = contract_rows(hidden[1], cotangents[0]).astype(jnp.bfloat16)
    grad_second_down = contract_rows(hidden[2], cotangents[1]).astype(jnp.bfloat16)
    dims = (((1,), (1,)), ((), ()))
    backs = (
        lax.dot_general(cotangents[0], first_down, dims, preferred_element_type=jnp.float32),
        lax.dot_general(cotangents[1], second_down, dims, preferred_element_type=jnp.float32),
    )
    back_full = lax.psum((backs[0], backs[1]), "split")
    first_dg, first_du = hidden_grads(back_full[0], values[2], values[3])
    second_dg, second_du = hidden_grads(back_full[1], values[4], values[5])
    grads_in = (first_dg, first_du, second_dg, second_du)
    outputs = tuple((contract_rows(gathered, item).astype(jnp.bfloat16) for item in grads_in))
    return (
        outputs[0],
        outputs[1],
        grad_first_down,
        outputs[2],
        outputs[3],
        grad_second_down,
        losses,
    )


def run(mp, split, *args):
    rows = args[0].shape[0] * mp
    if split == 4 and mp == 4 and args[0].shape[0] % 16 == 0 and rows % 64 == 0:
        return per_device_kernels(mp, *args)
    return per_device(*args)


def solution(mesh):
    placed = (
        P(("parts", "mp"), "split"),
        P("parts"),
        P(("parts", "split"), "mp"),
        P(("parts", "split"), "mp"),
        P(("parts", "mp"), "split"),
        P(("parts", "split"), "mp"),
        P(("parts", "split"), "mp"),
        P(("parts", "mp"), "split"),
        P(("parts", "split"), "mp"),
        P(("parts", "split"), "mp"),
        P(("parts", "mp"), "split"),
    )
    return jax.shard_map(
        functools.partial(run, mesh.shape["mp"], mesh.shape["split"]),
        mesh=mesh,
        in_specs=placed,
        out_specs=(
            P(("parts", "split"), "mp"),
            P(("parts", "split"), "mp"),
            P(("parts", "mp"), "split"),
            P(("parts", "split"), "mp"),
            P(("parts", "split"), "mp"),
            P(("parts", "mp"), "split"),
            P("parts"),
        ),
        check_vma=False,
    )
```

```python
import functools

import jax
import jax.numpy as jnp
from jax import lax
from jax.experimental import pallas as pl
from jax.experimental.pallas import tpu as pltpu
from jax.sharding import PartitionSpec as P

MESH = pl.DeviceIdType.MESH
VMEM = pl.BlockSpec(memory_space=pltpu.VMEM)
ANY = pl.BlockSpec(memory_space=pl.ANY)
TILE = 768
GRANT = 67043328

LEN = 64


def contract_rows(left, right):
    return lax.dot_general(
        left, right, (((0,), (0,)), ((), ())), preferred_element_type=jnp.float32
    )


def valid_rows(lengths, count):
    position = jnp.arange(count, dtype=jnp.int32)
    seq_ids = position // LEN
    within = position - seq_ids * LEN
    limit = jnp.sum(
        jnp.where(
            seq_ids[:, None] == jnp.arange(lengths.shape[0], dtype=jnp.int32)[None, :],
            lengths[None, :],
            0,
        ),
        axis=1,
    )
    return (within < limit).astype(jnp.float32)[:, None]


def activate(gate, up):
    return (jax.nn.silu(gate) * up).astype(jnp.bfloat16)


def hidden_grads(back, gate, up):
    sig = jax.nn.sigmoid(gate)
    dgate = (back * up * sig * (1.0 + gate * (1.0 - sig))).astype(jnp.bfloat16)
    dup = (back * gate * sig).astype(jnp.bfloat16)
    return (dgate, dup)


def view(spot):
    return spot[0].at[spot[1]] if isinstance(spot, tuple) else spot


class Move:
    def __init__(self, *args):
        self.args = args

    def build(self):
        src, dst, send, recv, at, device = self.args
        if device is None:
            return pltpu.make_async_copy(view(src), view(dst), recv.at[at])
        return pltpu.make_async_remote_copy(
            src_ref=view(src),
            dst_ref=view(dst),
            send_sem=send.at[at],
            recv_sem=recv.at[at],
            device_id=device,
            device_id_type=MESH,
        )

    def wait(self):
        self.build().wait()

    def wait_recv(self):
        self.build().wait_recv()

    def wait_send(self):
        self.build().wait_send()


class Links:
    def __init__(self, send, recv):
        self.send, self.recv, self.count, self.made = send, recv, 0, []

    def copy(self, src, dst, device=None):
        made = Move(src, dst, self.send, self.recv, self.count, device)
        self.count += 1
        made.build().start()
        self.made.append(made)
        return made

    def settle(self, made):
        made.wait_send()
        self.made.remove(made)

    def drain(self):
        for made in self.made:
            made.wait_send()


def greet(devices):
    barrier = pltpu.get_barrier_semaphore()
    for device in devices:
        pl.semaphore_signal(barrier, inc=1, device_id=device, device_id_type=MESH)
    pl.semaphore_wait(barrier, len(devices))


def cuts(width, shares):
    if width % 128:
        return [(0, width)]
    lanes, whole, made, taken, start = width // 128, sum(shares), [], 0, 0
    for share in shares:
        taken += share
        end = lanes * taken // whole * 128
        if end > start:
            made.append((start, end - start))
        start = end
    return made


def tiles(piece, body, tile=TILE):
    start, width = piece
    full = width // tile
    if full == 1:
        body(pl.ds(start, tile))
    elif full:

        @pl.loop(0, full)
        def _(i):
            body(pl.ds(pl.multiple_of(start + i * tile, 128), tile))

    if width % tile:
        body(pl.ds(start + full * tile, width % tile))


def four_places(axis):
    me = lax.axis_index(axis)
    chip, core = me // 2, me % 2
    sib = chip * 2 + (1 - core)
    far = (1 - chip) * 2 + core
    diag = (1 - chip) * 2 + (1 - core)
    return me, sib, far, diag


class Places:
    def __init__(self, axis, count):
        self.axis, self.count = axis, count
        self.me, self.sib, self.far, self.diag = self.ids = four_places(axis)
        self.rows = [rows_at(place, count) for place in self.ids]

    def to(self, k):
        return {self.axis: self.ids[k]}


def rows_at(block, count):
    return pl.ds(pl.multiple_of(block * count, 16), count)


def part(ref, piece, rows=slice(None)):
    return ref, (rows, pl.ds(*piece))


class Unit:
    def __init__(self, links, places, refs):
        self.links, self.places = links, places
        self.snd1, self.own, self.rcv1, self.snd2, self.rcv2 = refs
        self.half = self.own.shape[0] // 2
        self.width = self.own.shape[1]
        self.first, self.second = {}, {}

    def pass_on(self, piece):
        self.first[piece] = self.links.copy(
            part(self.snd1, piece), part(self.rcv1, piece), self.places.to(1)
        )

    def multiply(self, left, weight, flip, piece):
        pair = 2 * self.half

        def body(cols):
            if flip:
                right, dims = weight[cols, :], (((1,), (1,)), ((), ()))
            else:
                right, dims = weight[:, cols], (((1,), (0,)), ((), ()))
            out = lax.dot_general(left[...], right, dims, preferred_element_type=jnp.float32)
            self.snd1[:, cols] = out[:pair].astype(self.snd1.dtype)
            self.own[:, cols] = out[pair:]

        tiles(piece, body)
        self.pass_on(piece)

    def take(self, source, piece):
        me, sib, far, diag = self.places.rows
        half = self.half
        cols = pl.ds(*piece)
        for i, rows in enumerate((diag, sib)):
            self.snd1[i * half : (i + 1) * half, cols] = source[rows, cols].astype(self.snd1.dtype)
        for i, rows in enumerate((far, me)):
            self.own[i * half : (i + 1) * half, cols] = source[rows, cols]
        self.pass_on(piece)

    def forward(self, piece):
        self.first[piece].wait_recv()
        half = self.half

        def body(cols):
            both = self.own[:half, cols] + self.rcv1[:half, cols].astype(jnp.float32)
            self.snd2[:, cols] = both.astype(jnp.bfloat16)

        tiles(piece, body)
        self.second[piece] = self.links.copy(
            part(self.snd2, piece), part(self.rcv2, piece), self.places.to(2)
        )

    def ready(self, piece):
        self.second[piece].wait_recv()

    def value(self, cols):
        half = self.half
        return (
            self.own[half:, cols]
            + self.rcv1[half:, cols].astype(jnp.float32)
            + self.rcv2[:, cols].astype(jnp.float32)
        )

    def settle(self):
        for made in (*self.first.values(), *self.second.values()):
            self.links.settle(made)


class Exchange(Unit):
    def __init__(self, links, places, refs):
        super().__init__(links, places, (*refs[:3], None, None))
        self.snd2, self.rcv2 = refs[3], refs[4]

    def forward(self, piece):
        self.first[piece].wait_recv()
        half = self.half

        def body(cols):
            for k in range(2):
                rows = slice(k * half, (k + 1) * half)
                both = self.own[rows, cols] + self.rcv1[rows, cols]
                self.own[rows, cols] = both
                self.snd2[k][:, cols] = both.astype(jnp.bfloat16)

        tiles(piece, body)
        self.second[piece] = [
            self.links.copy(part(self.snd2[k], piece), part(self.rcv2[1 - k], piece), self.places.to(2))
            for k in range(2)
        ]

    def ready(self, piece):
        for made in self.second[piece]:
            made.wait_recv()

    def value(self, k, cols):
        rows = slice(k * self.half, (k + 1) * self.half)
        return self.own[rows, cols] + self.rcv2[k][:, cols].astype(jnp.float32)


def unit_scratch(rows, width, kind=jnp.float32):
    half, pair = rows // 4, rows // 2
    return [
        pltpu.VMEM((pair, width), kind),
        pltpu.VMEM((pair, width), jnp.float32),
        pltpu.VMEM((pair, width), kind),
        pltpu.VMEM((half, width), jnp.bfloat16),
        pltpu.VMEM((half, width), jnp.bfloat16),
    ]


class Spread:
    def __init__(self, links, ref, places, piece=None, source=None):
        self.links, self.places = links, places
        piece = (0, ref.shape[1]) if piece is None else piece
        mine = part(ref, piece, places.rows[0])
        self.theirs = part(ref, piece, places.rows[2])
        source = mine if source is None else source
        self.out = links.copy(source, mine, places.to(2))
        self.side = links.copy(source, mine, places.to(1))

    def relay(self):
        self.out.wait_recv()
        self.last = self.links.copy(self.theirs, self.theirs, self.places.to(1))

    def finish(self):
        self.side.wait_recv()
        self.last.wait_recv()


def arrange(dst, src, places):
    me, sib, far, diag = places.rows
    count = places.count
    for i, rows in enumerate((diag, sib, far, me)):
        dst[i * count : (i + 1) * count, :] = src[rows, :]


def row_scale(scale, lengths):
    position = lax.broadcasted_iota(jnp.int32, scale.shape, 0)
    seq_ids = position // LEN
    within = position - seq_ids * LEN
    limit, counted = jnp.zeros(scale.shape, jnp.int32), 0
    for i in range(lengths.shape[0]):
        length = lengths[i]
        limit = jnp.where(seq_ids == i, length, limit)
        counted = counted + length
    whole = jnp.full(scale.shape, counted, jnp.int32).astype(jnp.float32)
    scale[...] = jnp.where(within < limit, 2.0 / whole, 0.0)


def layer_kernel(flips, *refs):
    refs = iter(refs)

    def take(n):
        return [next(refs) for _ in range(n)]

    (tok, lengths), weights, downs = take(2), take(6), take(3)
    kept_out, loss = take(9), take(1)[0]
    gathered, xp, xq = take(3)
    hidden, grads, cots = take(3), take(4), take(2)
    near, away = take(4), take(4)
    target, diff, scale, part_sums, marked = take(5)
    unit_refs = [take(5) for _ in range(6)]
    ring_refs = [take(5) for _ in range(2)]
    send, recv, wsem, dsem, osem = take(5)

    links, loads, stores = Links(send, recv), Links(None, wsem), Links(None, osem)
    places, ring = Places("split", tok.shape[0]), Places("mp", tok.shape[0])
    mine, turn = places.rows[0], ring.rows[0]
    units = [Unit(links, places, r) for r in unit_refs]
    rings = [Unit(links, ring, r) for r in ring_refs]
    layers = ((2, (3, 6, 9, 9)), (0, (1,)), (1, (6, 5)))
    pieces = {layer: cuts(units[2 * layer].width, n) for layer, n in layers}
    out = []

    def project(*wbuf):
        waits = {}
        for layer, _ in layers:
            for piece in pieces[layer]:
                for i in (2 * layer, 2 * layer + 1):
                    src, dst = weights[i], wbuf[i]
                    if piece != (0, units[i].width):
                        at = (pl.ds(*piece), slice(None))
                        at = at if flips[i] else at[::-1]
                        src, dst = (src, at), (dst, at)
                    waits[i, piece] = loads.copy(src, dst)
        row_scale(scale, lengths)
        greet([spot.to(k) for spot in (places, ring) for k in (1, 2, 3)])
        moves = Spread(links, gathered, ring, source=tok)
        gathered[turn, :] = tok[...]
        moves.relay()
        moves.finish()
        out.append(stores.copy(gathered, kept_out[0]))
        arrange(xp, gathered, places)
        behind = None
        for layer, _ in layers:
            for piece in pieces[layer]:
                for i in (2 * layer, 2 * layer + 1):
                    waits[i, piece].wait()
                    units[i].multiply(xp, wbuf[i], flips[i], piece)
                    if behind is not None:
                        units[behind[0]].forward(behind[1])
                    behind = (i, piece) if layer != 1 else None

    pl.run_scoped(project, *[pltpu.VMEM(w.shape, jnp.bfloat16) for w in weights])

    def rest(*dbuf):
        waits = {}
        drops = Links(None, dsem)
        for layer, _ in layers:
            for piece in pieces[layer]:
                rows = pl.ds(*piece)
                src, dst = (downs[layer], rows), (dbuf[layer], rows)
                waits[layer, piece] = drops.copy(src, dst)
        spreads = {}

        def activate(layer, piece):
            gate, up = units[2 * layer], units[2 * layer + 1]
            gate.ready(piece)
            up.ready(piece)

            def body(cols):
                g, u = gate.value(cols), up.value(cols)
                sig = jax.nn.sigmoid(g)
                slope = g * sig
                hidden[layer][mine, cols] = (slope * u).astype(jnp.bfloat16)
                if layer < 2:
                    bend = u * sig * (1.0 + g * (1.0 - sig))
                    gate.own[gate.half :, cols] = bend
                    up.own[up.half :, cols] = slope
                    near[2 * layer][:, cols] = bend.astype(jnp.bfloat16)
                    near[2 * layer + 1][:, cols] = slope.astype(jnp.bfloat16)

            tiles(piece, body)
            spreads[layer, piece] = Spread(links, hidden[layer], places, piece)

        wide = (0, target.shape[1])

        def project_down(layer, piece, first, dst, sign):
            spreads[layer, piece].finish()
            waits[layer, piece].wait()
            rows = pl.ds(*piece)

            def body(cols):
                out = jnp.dot(
                    hidden[layer][:, rows],
                    dbuf[layer][rows, cols],
                    preferred_element_type=jnp.float32,
                )
                if first is None:
                    dst[:, cols] += out
                elif sign:
                    dst[:, cols] = out
                else:
                    dst[:, cols] = out - first[:, cols]

            tiles(wide, body, 1280)

        halves = cuts(target.shape[1], (1, 1))
        for piece in pieces[2]:
            activate(2, piece)
        for piece in pieces[0]:
            activate(0, piece)
        for piece in pieces[1]:
            for i in (2, 3):
                units[i].forward(piece)
        for piece in pieces[2]:
            spreads[2, piece].relay()
        for n, piece in enumerate(pieces[2]):
            project_down(2, piece, None if n else target, target, n == 0)
        for piece in pieces[0]:
            spreads[0, piece].relay()
        for n, piece in enumerate(pieces[0]):
            project_down(0, piece, None if n else target, diff, False)
        out.append(stores.copy(hidden[0], kept_out[1]))
        for half in halves:
            rings[0].take(diff, half)
        for piece in pieces[1]:
            activate(1, piece)
        lent = [links.copy(near[i], away[i], places.to(2)) for i in range(4)]
        for n, piece in enumerate(pieces[1]):
            spreads[1, piece].relay()
            if n < len(halves):
                rings[0].forward(halves[n])
        for half in halves[len(pieces[1]) :]:
            rings[0].forward(half)
        for n, piece in enumerate(pieces[1]):
            project_down(1, piece, None if n else target, target, False)
        out.append(stores.copy(hidden[1], kept_out[2]))
        for half in halves:
            rings[1].take(target, half)

        factor = scale[turn, 0:1]
        turns, sums = ([], []), [0.0, 0.0]

        def cotangent(i, half):
            rings[i].ready(half)
            cols = pl.ds(*half)
            total = rings[i].value(cols)
            scaled = factor * total
            cots[i][turn, cols] = scaled.astype(jnp.bfloat16)
            turns[i].append(Spread(links, cots[i], ring, half))
            sums[i] = sums[i] + 0.5 * jnp.sum(scaled * total, keepdims=True)

        back, parcels = [], [[], []]
        for i in range(2):
            gate, up = units[2 * i], units[2 * i + 1]
            pair = ((up.snd2, gate.snd2), (up.rcv2, gate.rcv2))
            back.append(Exchange(links, places, (gate.snd1, up.snd1, gate.rcv1, *pair)))
            gate.settle()
            up.settle()

        def differentiate(i, piece):
            back[i].ready(piece)
            half = back[i].half

            def body(cols):
                for k, rows in enumerate((places.rows[2], mine)):
                    value = back[i].value(k, cols)
                    for j in range(2):
                        factor = units[2 * i + j].own[half:, cols] if k else away[2 * i + j][:, cols]
                        out = value * factor.astype(jnp.float32)
                        grads[2 * i + j][rows, cols] = out.astype(jnp.bfloat16)

            tiles(piece, body)
            for j in range(2):
                for rows in (places.rows[2], mine):
                    spot = part(grads[2 * i + j], piece, rows)
                    parcels[i].append(links.copy(spot, spot, places.to(1)))

        def collect(i):
            for made in parcels[i]:
                made.wait_recv()
            for j in range(2):
                out.append(stores.copy(grads[2 * i + j], kept_out[5 + 2 * i + j]))

        def back_project(i, left):
            for made in turns[i]:
                made.finish()
            out.append(stores.copy(cots[i], kept_out[3 + i]))
            arrange(left, cots[i], places)
            for piece in pieces[i]:
                back[i].multiply(left, dbuf[i], True, piece)

        for half in halves:
            cotangent(0, half)
            rings[1].forward(half)
        for made in turns[0]:
            made.relay()
        cotangent(1, halves[0])
        back_project(0, xp)
        for half in halves[1:]:
            cotangent(1, half)
        for piece in pieces[0]:
            back[0].forward(piece)
        for made in turns[1]:
            made.relay()
        row = lax.broadcasted_iota(jnp.int32, part_sums.shape[1:], 0)
        part_sums[0] = jnp.where(row == 0, sums[0], sums[1])
        parts = [
            links.copy((part_sums, 0), (part_sums, k), ring.to(k)) for k in (1, 2, 3)
        ]
        back_project(1, xq)
        for piece in pieces[1]:
            back[1].forward(piece)
        for made in lent:
            made.wait_recv()
        for piece in pieces[0]:
            differentiate(0, piece)
        for move in parts:
            move.wait_recv()
        marked[0] = part_sums[0] + part_sums[1] + part_sums[2] + part_sums[3]
        marks = [
            links.copy((marked, 0), (marked, k), places.to(k)) for k in (1, 2, 3)
        ]
        collect(0)
        for piece in pieces[1]:
            differentiate(1, piece)
        for mark in marks:
            mark.wait_recv()
        loss[...] = marked[0] + marked[1] + marked[2] + marked[3]
        collect(1)
        for made in out:
            made.wait()
        links.drain()

    pl.run_scoped(rest, *[pltpu.VMEM(d.shape, jnp.bfloat16) for d in downs])


def layer_call(mp, tokens, lengths, weights, downs, flips):
    block, depth = tokens.shape
    rows = block * mp
    widths = [d.shape[0] for d in downs]
    shape, bf16, f32 = jax.ShapeDtypeStruct, jnp.bfloat16, jnp.float32
    outs = [shape((rows, depth), bf16)]
    outs += [shape((rows, widths[i]), bf16) for i in range(2)]
    outs += [shape((rows, depth), bf16)] * 2
    outs += [shape((rows, widths[i // 2]), bf16) for i in range(4)]
    outs.append(shape((8, 128), f32))
    scratch = [pltpu.VMEM((rows, depth), bf16)] * 3
    scratch += [pltpu.VMEM((rows, w), bf16) for w in widths]
    scratch += [pltpu.VMEM((rows, widths[i // 2]), bf16) for i in range(4)]
    scratch += [pltpu.VMEM((rows, depth), bf16)] * 2
    scratch += [pltpu.VMEM((block, widths[i // 2]), bf16) for i in range(4)] * 2
    scratch += [pltpu.VMEM((rows, depth), f32)] * 2
    scratch += [pltpu.VMEM((rows, 128), f32)]
    scratch += [pltpu.VMEM((4, 8, 128), f32)] * 2
    for i in range(6):
        scratch += unit_scratch(rows, widths[i // 2])
    for _ in range(2):
        scratch += unit_scratch(rows, depth, bf16)
    copies = 160
    scratch += [pltpu.SemaphoreType.DMA((copies,))] * 2
    scratch += [pltpu.SemaphoreType.DMA((24,))] * 3
    return pl.pallas_call(
        functools.partial(layer_kernel, flips),
        out_shape=outs,
        in_specs=[VMEM, pl.BlockSpec(memory_space=pltpu.SMEM)] + [ANY] * 9,
        out_specs=[ANY] * 9 + [VMEM],
        scratch_shapes=scratch,
        compiler_params=pltpu.CompilerParams(
            collective_id=0, has_side_effects=True, vmem_limit_bytes=GRANT
        ),
    )(tokens, lengths, *weights, *downs)


def gradient_kernel(jobs, *refs):
    refs = iter(refs)

    def take(n):
        return [next(refs) for _ in range(n)]

    sources, loss, outs, losses = take(9), take(1)[0], take(len(jobs)), take(1)[0]
    held, made = take(9), take(len(jobs))
    isem, osem = take(2)
    order = list(dict.fromkeys(i for job in jobs for i in job))
    loads = {i: pltpu.make_async_copy(sources[i], held[i], isem.at[i]) for i in order}
    for i in order:
        loads[i].start()
    for i in range(losses.shape[0]):
        losses[i] = loss[i, 0]
    for j, job in enumerate(jobs):
        for i in job:
            if i in loads:
                loads.pop(i).wait()
        left, right, dst = held[job[0]], held[job[1]], made[j]
        height, width = dst.shape
        step = -(-height // 256) * 128
        for start in range(0, height, step):
            rows = pl.ds(start, min(step, height - start))
            for at in range(0, width, 256):
                cols = pl.ds(at, min(256, width - at))
                dst[rows, cols] = contract_rows(left[:, rows], right[:, cols]).astype(dst.dtype)
            pltpu.make_async_copy(dst.at[rows], outs[j].at[rows], osem.at[j]).start()
    for j in range(len(jobs)):
        pltpu.make_async_copy(made[j], outs[j], osem.at[j]).wait()


def gradient_call(arrays, loss, jobs, students):
    shape = jax.ShapeDtypeStruct
    outs = [shape((arrays[a].shape[1], arrays[b].shape[1]), jnp.bfloat16) for a, b in jobs]
    smem = pl.BlockSpec(memory_space=pltpu.SMEM)
    scratch = [pltpu.VMEM(item.shape, item.dtype) for item in (*arrays, *outs)]
    scratch += [pltpu.SemaphoreType.DMA((len(arrays),)), pltpu.SemaphoreType.DMA((len(jobs),))]
    return pl.pallas_call(
        functools.partial(gradient_kernel, jobs),
        out_shape=outs + [shape((students,), jnp.float32)],
        in_specs=[ANY] * len(arrays) + [smem],
        out_specs=[ANY] * len(jobs) + [smem],
        scratch_shapes=scratch,
        compiler_params=pltpu.CompilerParams(vmem_limit_bytes=GRANT),
    )(*arrays, loss)


def per_device_kernels(
    mp,
    tokens,
    lengths,
    teacher_gate,
    teacher_up,
    teacher_down,
    first_gate,
    first_up,
    first_down,
    second_gate,
    second_up,
    second_down,
):
    weights, flips = [], []
    for w in (first_gate, first_up, second_gate, second_up, teacher_gate, teacher_up):
        flip = w.shape[1] % 128 != 0
        flips.append(flip)
        weights.append(w.T if flip else w)
    *arrays, loss = layer_call(
        mp, tokens, lengths, weights, (first_down, second_down, teacher_down), tuple(flips)
    )
    jobs = [(1, 3), (2, 4)]
    jobs += [(5 + i, 0) if flips[i] else (0, 5 + i) for i in range(4)]
    made = gradient_call(arrays, loss, tuple(jobs), 2)
    ins = [out.T if flip else out for out, flip in zip(made[2:6], flips)]
    return ins[0], ins[1], made[0], ins[2], ins[3], made[1], made[6]


def per_device(
    tokens,
    lengths,
    teacher_gate,
    teacher_up,
    teacher_down,
    first_gate,
    first_up,
    first_down,
    second_gate,
    second_up,
    second_down,
):
    gathered = lax.all_gather(tokens, "mp", axis=0, tiled=True)
    total_rows = gathered.shape[0]

    def project(weight):
        return jnp.dot(gathered, weight, preferred_element_type=jnp.float32)

    partials = (
        project(teacher_gate),
        project(teacher_up),
        project(first_gate),
        project(first_up),
        project(second_gate),
        project(second_up),
    )
    values = lax.psum(
        (partials[0], partials[1], partials[2], partials[3], partials[4], partials[5]), "split"
    )
    hidden = (
        activate(values[0], values[1]),
        activate(values[2], values[3]),
        activate(values[4], values[5]),
    )
    target = jnp.dot(hidden[0], teacher_down, preferred_element_type=jnp.float32)
    diffs = (
        jnp.dot(hidden[1], first_down, preferred_element_type=jnp.float32) - target,
        jnp.dot(hidden[2], second_down, preferred_element_type=jnp.float32) - target,
    )
    counted = jnp.sum(lengths).astype(jnp.float32)
    summed = lax.psum((diffs[0], diffs[1]), "mp")
    mask = valid_rows(lengths, total_rows)
    partial_loss = (
        jnp.stack([jnp.sum(mask * summed[0] * summed[0]), jnp.sum(mask * summed[1] * summed[1])])
        / counted
    )
    losses = lax.psum(partial_loss, "split")
    cotangents = (
        (2.0 * mask * summed[0] / counted).astype(jnp.bfloat16),
        (2.0 * mask * summed[1] / counted).astype(jnp.bfloat16),
    )
    grad_first_down = contract_rows(hidden[1], cotangents[0]).astype(jnp.bfloat16)
    grad_second_down = contract_rows(hidden[2], cotangents[1]).astype(jnp.bfloat16)
    dims = (((1,), (1,)), ((), ()))
    backs = (
        lax.dot_general(cotangents[0], first_down, dims, preferred_element_type=jnp.float32),
        lax.dot_general(cotangents[1], second_down, dims, preferred_element_type=jnp.float32),
    )
    back_full = lax.psum((backs[0], backs[1]), "split")
    first_dg, first_du = hidden_grads(back_full[0], values[2], values[3])
    second_dg, second_du = hidden_grads(back_full[1], values[4], values[5])
    grads_in = (first_dg, first_du, second_dg, second_du)
    outputs = tuple((contract_rows(gathered, item).astype(jnp.bfloat16) for item in grads_in))
    return (
        outputs[0],
        outputs[1],
        grad_first_down,
        outputs[2],
        outputs[3],
        grad_second_down,
        losses,
    )


def run(mp, split, *args):
    rows = args[0].shape[0] * mp
    if split == 4 and mp == 4 and args[0].shape[0] % 16 == 0 and rows % 64 == 0:
        return per_device_kernels(mp, *args)
    return per_device(*args)


def solution(mesh):
    placed = (
        P(("parts", "mp"), "split"),
        P("parts"),
        P(("parts", "split"), "mp"),
        P(("parts", "split"), "mp"),
        P(("parts", "mp"), "split"),
        P(("parts", "split"), "mp"),
        P(("parts", "split"), "mp"),
        P(("parts", "mp"), "split"),
        P(("parts", "split"), "mp"),
        P(("parts", "split"), "mp"),
        P(("parts", "mp"), "split"),
    )
    return jax.shard_map(
        functools.partial(run, mesh.shape["mp"], mesh.shape["split"]),
        mesh=mesh,
        in_specs=placed,
        out_specs=(
            P(("parts", "split"), "mp"),
            P(("parts", "split"), "mp"),
            P(("parts", "mp"), "split"),
            P(("parts", "split"), "mp"),
            P(("parts", "split"), "mp"),
            P(("parts", "mp"), "split"),
            P("parts"),
        ),
        check_vma=False,
    )
```

```python
import functools

import jax
import jax.numpy as jnp
from jax import lax
from jax.experimental import pallas as pl
from jax.experimental.pallas import tpu as pltpu
from jax.sharding import PartitionSpec as P

MESH = pl.DeviceIdType.MESH
VMEM = pl.BlockSpec(memory_space=pltpu.VMEM)
ANY = pl.BlockSpec(memory_space=pl.ANY)
TILE = 1152
GRANT = 67043328

LEN = 64


def contract_rows(left, right):
    return lax.dot_general(
        left, right, (((0,), (0,)), ((), ())), preferred_element_type=jnp.float32
    )


def valid_rows(lengths, count):
    position = jnp.arange(count, dtype=jnp.int32)
    seq_ids = position // LEN
    within = position - seq_ids * LEN
    limit = jnp.sum(
        jnp.where(
            seq_ids[:, None] == jnp.arange(lengths.shape[0], dtype=jnp.int32)[None, :],
            lengths[None, :],
            0,
        ),
        axis=1,
    )
    return (within < limit).astype(jnp.float32)[:, None]


def activate(gate, up):
    return (jax.nn.silu(gate) * up).astype(jnp.bfloat16)


def hidden_grads(back, gate, up):
    sig = jax.nn.sigmoid(gate)
    dgate = (back * up * sig * (1.0 + gate * (1.0 - sig))).astype(jnp.bfloat16)
    dup = (back * gate * sig).astype(jnp.bfloat16)
    return (dgate, dup)


def view(spot):
    return spot[0].at[spot[1]] if isinstance(spot, tuple) else spot


class Move:
    def __init__(self, *args):
        self.args = args

    def build(self):
        src, dst, send, recv, at, device = self.args
        if device is None:
            return pltpu.make_async_copy(view(src), view(dst), recv.at[at])
        return pltpu.make_async_remote_copy(
            src_ref=view(src),
            dst_ref=view(dst),
            send_sem=send.at[at],
            recv_sem=recv.at[at],
            device_id=device,
            device_id_type=MESH,
        )

    def wait(self):
        self.build().wait()

    def wait_recv(self):
        self.build().wait_recv()

    def wait_send(self):
        self.build().wait_send()


class Links:
    def __init__(self, send, recv):
        self.send, self.recv, self.count, self.made = send, recv, 0, []

    def copy(self, src, dst, device=None):
        made = Move(src, dst, self.send, self.recv, self.count, device)
        self.count += 1
        made.build().start()
        self.made.append(made)
        return made

    def settle(self, made):
        made.wait_send()
        self.made.remove(made)

    def drain(self):
        for made in self.made:
            made.wait_send()


def greet(devices):
    barrier = pltpu.get_barrier_semaphore()
    for device in devices:
        pl.semaphore_signal(barrier, inc=1, device_id=device, device_id_type=MESH)
    pl.semaphore_wait(barrier, len(devices))


def cuts(width, shares):
    if width % 128:
        return [(0, width)]
    lanes, whole, made, taken, start = width // 128, sum(shares), [], 0, 0
    for share in shares:
        taken += share
        end = lanes * taken // whole * 128
        if end > start:
            made.append((start, end - start))
        start = end
    return made


def tiles(piece, body, tile=TILE):
    start, width = piece
    full = width // tile
    if full == 1:
        body(pl.ds(start, tile))
    elif full:

        @pl.loop(0, full)
        def _(i):
            body(pl.ds(pl.multiple_of(start + i * tile, 128), tile))

    if width % tile:
        body(pl.ds(start + full * tile, width % tile))


def four_places(axis):
    me = lax.axis_index(axis)
    chip, core = me // 2, me % 2
    sib = chip * 2 + (1 - core)
    far = (1 - chip) * 2 + core
    diag = (1 - chip) * 2 + (1 - core)
    return me, sib, far, diag


class Places:
    def __init__(self, axis, count):
        self.axis, self.count = axis, count
        self.me, self.sib, self.far, self.diag = self.ids = four_places(axis)
        self.rows = [rows_at(place, count) for place in self.ids]

    def to(self, k):
        return {self.axis: self.ids[k]}


def rows_at(block, count):
    return pl.ds(pl.multiple_of(block * count, 16), count)


def part(ref, piece, rows=slice(None)):
    return ref, (rows, pl.ds(*piece))


class Unit:
    def __init__(self, links, places, refs):
        self.links, self.places = links, places
        self.snd1, self.own, self.rcv1, self.snd2, self.rcv2 = refs
        self.half = self.own.shape[0] // 2
        self.width = self.own.shape[1]
        self.first, self.second = {}, {}

    def pass_on(self, piece):
        self.first[piece] = self.links.copy(
            part(self.snd1, piece), part(self.rcv1, piece), self.places.to(1)
        )

    def multiply(self, left, weight, flip, piece):
        pair = 2 * self.half

        def body(cols):
            if flip:
                right, dims = weight[cols, :], (((1,), (1,)), ((), ()))
            else:
                right, dims = weight[:, cols], (((1,), (0,)), ((), ()))
            out = lax.dot_general(left[...], right, dims, preferred_element_type=jnp.float32)
            self.snd1[:, cols] = out[:pair].astype(self.snd1.dtype)
            self.own[:, cols] = out[pair:]

        tiles(piece, body)
        self.pass_on(piece)

    def take(self, source, piece):
        me, sib, far, diag = self.places.rows
        half = self.half
        cols = pl.ds(*piece)
        for i, rows in enumerate((diag, sib)):
            self.snd1[i * half : (i + 1) * half, cols] = source[rows, cols].astype(self.snd1.dtype)
        for i, rows in enumerate((far, me)):
            self.own[i * half : (i + 1) * half, cols] = source[rows, cols]
        self.pass_on(piece)

    def forward(self, piece):
        self.first[piece].wait_recv()
        half = self.half

        def body(cols):
            both = self.own[:half, cols] + self.rcv1[:half, cols].astype(jnp.float32)
            self.snd2[:, cols] = both.astype(jnp.bfloat16)

        tiles(piece, body)
        self.second[piece] = self.links.copy(
            part(self.snd2, piece), part(self.rcv2, piece), self.places.to(2)
        )

    def ready(self, piece):
        self.second[piece].wait_recv()

    def value(self, cols):
        half = self.half
        return (
            self.own[half:, cols]
            + self.rcv1[half:, cols].astype(jnp.float32)
            + self.rcv2[:, cols].astype(jnp.float32)
        )

    def settle(self):
        for made in (*self.first.values(), *self.second.values()):
            self.links.settle(made)


class Exchange(Unit):
    def __init__(self, links, places, refs):
        super().__init__(links, places, (*refs[:3], None, None))
        self.snd2, self.rcv2 = refs[3], refs[4]

    def forward(self, piece):
        self.first[piece].wait_recv()
        half = self.half

        def body(cols):
            for k in range(2):
                rows = slice(k * half, (k + 1) * half)
                both = self.own[rows, cols] + self.rcv1[rows, cols]
                self.own[rows, cols] = both
                self.snd2[k][:, cols] = both.astype(jnp.bfloat16)

        tiles(piece, body)
        self.second[piece] = [
            self.links.copy(part(self.snd2[k], piece), part(self.rcv2[1 - k], piece), self.places.to(2))
            for k in range(2)
        ]

    def ready(self, piece):
        for made in self.second[piece]:
            made.wait_recv()

    def value(self, k, cols):
        rows = slice(k * self.half, (k + 1) * self.half)
        return self.own[rows, cols] + self.rcv2[k][:, cols].astype(jnp.float32)


def unit_scratch(rows, width, kind=jnp.float32):
    half, pair = rows // 4, rows // 2
    return [
        pltpu.VMEM((pair, width), kind),
        pltpu.VMEM((pair, width), jnp.float32),
        pltpu.VMEM((pair, width), kind),
        pltpu.VMEM((half, width), jnp.bfloat16),
        pltpu.VMEM((half, width), jnp.bfloat16),
    ]


class Spread:
    def __init__(self, links, ref, places, piece=None, source=None):
        self.links, self.places = links, places
        piece = (0, ref.shape[1]) if piece is None else piece
        mine = part(ref, piece, places.rows[0])
        self.theirs = part(ref, piece, places.rows[2])
        source = mine if source is None else source
        self.out = links.copy(source, mine, places.to(2))
        self.side = links.copy(source, mine, places.to(1))

    def relay(self):
        self.out.wait_recv()
        self.last = self.links.copy(self.theirs, self.theirs, self.places.to(1))

    def finish(self):
        self.side.wait_recv()
        self.last.wait_recv()


def arrange(dst, src, places):
    me, sib, far, diag = places.rows
    count = places.count
    for i, rows in enumerate((diag, sib, far, me)):
        dst[i * count : (i + 1) * count, :] = src[rows, :]


def row_scale(scale, lengths):
    position = lax.broadcasted_iota(jnp.int32, scale.shape, 0)
    seq_ids = position // LEN
    within = position - seq_ids * LEN
    limit, counted = jnp.zeros(scale.shape, jnp.int32), 0
    for i in range(lengths.shape[0]):
        length = lengths[i]
        limit = jnp.where(seq_ids == i, length, limit)
        counted = counted + length
    whole = jnp.full(scale.shape, counted, jnp.int32).astype(jnp.float32)
    scale[...] = jnp.where(within < limit, 2.0 / whole, 0.0)


def layer_kernel(flips, *refs):
    refs = iter(refs)

    def take(n):
        return [next(refs) for _ in range(n)]

    (tok, lengths), weights, downs = take(2), take(6), take(3)
    kept_out, loss = take(9), take(1)[0]
    gathered, xp, xq = take(3)
    hidden, grads, cots = take(3), take(4), take(2)
    near, away = take(4), take(4)
    target, diff, scale, part_sums, marked = take(5)
    unit_refs = [take(5) for _ in range(6)]
    ring_refs = [take(5) for _ in range(2)]
    send, recv, wsem, dsem, osem = take(5)

    links, loads, stores = Links(send, recv), Links(None, wsem), Links(None, osem)
    places, ring = Places("split", tok.shape[0]), Places("mp", tok.shape[0])
    mine, turn = places.rows[0], ring.rows[0]
    units = [Unit(links, places, r) for r in unit_refs]
    rings = [Unit(links, ring, r) for r in ring_refs]
    layers = ((2, (3, 6, 9, 9)), (0, (1,)), (1, (7, 4)))
    pieces = {layer: cuts(units[2 * layer].width, n) for layer, n in layers}
    out = []

    def project(*wbuf):
        waits = {}
        for layer, _ in layers:
            for piece in pieces[layer]:
                for i in (2 * layer, 2 * layer + 1):
                    src, dst = weights[i], wbuf[i]
                    if piece != (0, units[i].width):
                        at = (pl.ds(*piece), slice(None))
                        at = at if flips[i] else at[::-1]
                        src, dst = (src, at), (dst, at)
                    waits[i, piece] = loads.copy(src, dst)
        row_scale(scale, lengths)
        greet([spot.to(k) for spot in (places, ring) for k in (1, 2, 3)])
        moves = Spread(links, gathered, ring, source=tok)
        gathered[turn, :] = tok[...]
        moves.relay()
        moves.finish()
        out.append(stores.copy(gathered, kept_out[0]))
        arrange(xp, gathered, places)
        behind = None
        for layer, _ in layers:
            for piece in pieces[layer]:
                for i in (2 * layer, 2 * layer + 1):
                    waits[i, piece].wait()
                    units[i].multiply(xp, wbuf[i], flips[i], piece)
                    if behind is not None:
                        units[behind[0]].forward(behind[1])
                    behind = (i, piece) if layer != 1 else None

    pl.run_scoped(project, *[pltpu.VMEM(w.shape, jnp.bfloat16) for w in weights])

    def rest(*dbuf):
        waits = {}
        drops = Links(None, dsem)
        for layer, _ in layers:
            for piece in pieces[layer]:
                rows = pl.ds(*piece)
                src, dst = (downs[layer], rows), (dbuf[layer], rows)
                waits[layer, piece] = drops.copy(src, dst)
        spreads = {}

        def activate(layer, piece):
            gate, up = units[2 * layer], units[2 * layer + 1]
            gate.ready(piece)
            up.ready(piece)

            def body(cols):
                g, u = gate.value(cols), up.value(cols)
                sig = jax.nn.sigmoid(g)
                slope = g * sig
                hidden[layer][mine, cols] = (slope * u).astype(jnp.bfloat16)
                if layer < 2:
                    bend = u * sig * (1.0 + g * (1.0 - sig))
                    gate.own[gate.half :, cols] = bend
                    up.own[up.half :, cols] = slope
                    near[2 * layer][:, cols] = bend.astype(jnp.bfloat16)
                    near[2 * layer + 1][:, cols] = slope.astype(jnp.bfloat16)

            tiles(piece, body)
            spreads[layer, piece] = Spread(links, hidden[layer], places, piece)

        wide = (0, target.shape[1])

        def project_down(layer, piece, first, dst, sign):
            spreads[layer, piece].finish()
            waits[layer, piece].wait()
            rows = pl.ds(*piece)

            def body(cols):
                out = jnp.dot(
                    hidden[layer][:, rows],
                    dbuf[layer][rows, cols],
                    preferred_element_type=jnp.float32,
                )
                if first is None:
                    dst[:, cols] += out
                elif sign:
                    dst[:, cols] = out
                else:
                    dst[:, cols] = out - first[:, cols]

            tiles(wide, body, 1280)

        halves = cuts(target.shape[1], (1, 1))
        for piece in pieces[2]:
            activate(2, piece)
        for piece in pieces[0]:
            activate(0, piece)
        for piece in pieces[1]:
            for i in (2, 3):
                units[i].forward(piece)
        for piece in pieces[2]:
            spreads[2, piece].relay()
        for n, piece in enumerate(pieces[2]):
            project_down(2, piece, None if n else target, target, n == 0)
        for piece in pieces[0]:
            spreads[0, piece].relay()
        for n, piece in enumerate(pieces[0]):
            project_down(0, piece, None if n else target, diff, False)
        out.append(stores.copy(hidden[0], kept_out[1]))
        for half in halves:
            rings[0].take(diff, half)
        for piece in pieces[1]:
            activate(1, piece)
        lent = [links.copy(near[i], away[i], places.to(2)) for i in range(4)]
        for n, piece in enumerate(pieces[1]):
            spreads[1, piece].relay()
            if n < len(halves):
                rings[0].forward(halves[n])
        for half in halves[len(pieces[1]) :]:
            rings[0].forward(half)
        for n, piece in enumerate(pieces[1]):
            project_down(1, piece, None if n else target, target, False)
        out.append(stores.copy(hidden[1], kept_out[2]))
        for half in halves:
            rings[1].take(target, half)

        factor = scale[turn, 0:1]
        turns, sums = ([], []), [0.0, 0.0]

        def cotangent(i, half):
            rings[i].ready(half)
            cols = pl.ds(*half)
            total = rings[i].value(cols)
            scaled = factor * total
            cots[i][turn, cols] = scaled.astype(jnp.bfloat16)
            turns[i].append(Spread(links, cots[i], ring, half))
            sums[i] = sums[i] + 0.5 * jnp.sum(scaled * total, keepdims=True)

        back, parcels = [], [[], []]
        for i in range(2):
            gate, up = units[2 * i], units[2 * i + 1]
            pair = ((up.snd2, gate.snd2), (up.rcv2, gate.rcv2))
            back.append(Exchange(links, places, (gate.snd1, up.snd1, gate.rcv1, *pair)))
            gate.settle()
            up.settle()

        def differentiate(i, piece):
            back[i].ready(piece)
            half = back[i].half

            def body(cols):
                for k, rows in enumerate((places.rows[2], mine)):
                    value = back[i].value(k, cols)
                    for j in range(2):
                        factor = units[2 * i + j].own[half:, cols] if k else away[2 * i + j][:, cols]
                        out = value * factor.astype(jnp.float32)
                        grads[2 * i + j][rows, cols] = out.astype(jnp.bfloat16)

            tiles(piece, body)
            for j in range(2):
                for rows in (places.rows[2], mine):
                    spot = part(grads[2 * i + j], piece, rows)
                    parcels[i].append(links.copy(spot, spot, places.to(1)))

        def collect(i):
            for made in parcels[i]:
                made.wait_recv()
            for j in range(2):
                out.append(stores.copy(grads[2 * i + j], kept_out[5 + 2 * i + j]))

        def back_project(i, left):
            for made in turns[i]:
                made.finish()
            out.append(stores.copy(cots[i], kept_out[3 + i]))
            arrange(left, cots[i], places)
            for piece in pieces[i]:
                back[i].multiply(left, dbuf[i], True, piece)

        for half in halves:
            cotangent(0, half)
            rings[1].forward(half)
        for made in turns[0]:
            made.relay()
        cotangent(1, halves[0])
        back_project(0, xp)
        for half in halves[1:]:
            cotangent(1, half)
        for piece in pieces[0]:
            back[0].forward(piece)
        for made in turns[1]:
            made.relay()
        row = lax.broadcasted_iota(jnp.int32, part_sums.shape[1:], 0)
        part_sums[0] = jnp.where(row == 0, sums[0], sums[1])
        parts = [
            links.copy((part_sums, 0), (part_sums, k), ring.to(k)) for k in (1, 2, 3)
        ]
        back_project(1, xq)
        for piece in pieces[1]:
            back[1].forward(piece)
        for made in lent:
            made.wait_recv()
        for piece in pieces[0]:
            differentiate(0, piece)
        for move in parts:
            move.wait_recv()
        marked[0] = part_sums[0] + part_sums[1] + part_sums[2] + part_sums[3]
        marks = [
            links.copy((marked, 0), (marked, k), places.to(k)) for k in (1, 2, 3)
        ]
        collect(0)
        for piece in pieces[1]:
            differentiate(1, piece)
        for mark in marks:
            mark.wait_recv()
        loss[...] = marked[0] + marked[1] + marked[2] + marked[3]
        collect(1)
        for made in out:
            made.wait()
        links.drain()

    pl.run_scoped(rest, *[pltpu.VMEM(d.shape, jnp.bfloat16) for d in downs])


def layer_call(mp, tokens, lengths, weights, downs, flips):
    block, depth = tokens.shape
    rows = block * mp
    widths = [d.shape[0] for d in downs]
    shape, bf16, f32 = jax.ShapeDtypeStruct, jnp.bfloat16, jnp.float32
    outs = [shape((rows, depth), bf16)]
    outs += [shape((rows, widths[i]), bf16) for i in range(2)]
    outs += [shape((rows, depth), bf16)] * 2
    outs += [shape((rows, widths[i // 2]), bf16) for i in range(4)]
    outs.append(shape((8, 128), f32))
    scratch = [pltpu.VMEM((rows, depth), bf16)] * 3
    scratch += [pltpu.VMEM((rows, w), bf16) for w in widths]
    scratch += [pltpu.VMEM((rows, widths[i // 2]), bf16) for i in range(4)]
    scratch += [pltpu.VMEM((rows, depth), bf16)] * 2
    scratch += [pltpu.VMEM((block, widths[i // 2]), bf16) for i in range(4)] * 2
    scratch += [pltpu.VMEM((rows, depth), f32)] * 2
    scratch += [pltpu.VMEM((rows, 128), f32)]
    scratch += [pltpu.VMEM((4, 8, 128), f32)] * 2
    for i in range(6):
        scratch += unit_scratch(rows, widths[i // 2])
    for _ in range(2):
        scratch += unit_scratch(rows, depth, bf16)
    copies = 160
    scratch += [pltpu.SemaphoreType.DMA((copies,))] * 2
    scratch += [pltpu.SemaphoreType.DMA((24,))] * 3
    return pl.pallas_call(
        functools.partial(layer_kernel, flips),
        out_shape=outs,
        in_specs=[VMEM, pl.BlockSpec(memory_space=pltpu.SMEM)] + [ANY] * 9,
        out_specs=[ANY] * 9 + [VMEM],
        scratch_shapes=scratch,
        compiler_params=pltpu.CompilerParams(
            collective_id=0, has_side_effects=True, vmem_limit_bytes=GRANT
        ),
    )(tokens, lengths, *weights, *downs)


def gradient_kernel(jobs, *refs):
    refs = iter(refs)

    def take(n):
        return [next(refs) for _ in range(n)]

    sources, loss, outs, losses = take(9), take(1)[0], take(len(jobs)), take(1)[0]
    held, made = take(9), take(len(jobs))
    isem, osem = take(2)
    order = list(dict.fromkeys(i for job in jobs for i in job))
    loads = {i: pltpu.make_async_copy(sources[i], held[i], isem.at[i]) for i in order}
    for i in order:
        loads[i].start()
    for i in range(losses.shape[0]):
        losses[i] = loss[i, 0]
    for j, job in enumerate(jobs):
        for i in job:
            if i in loads:
                loads.pop(i).wait()
        left, right, dst = held[job[0]], held[job[1]], made[j]
        height, width = dst.shape
        step = -(-height // 256) * 128
        for start in range(0, height, step):
            rows = pl.ds(start, min(step, height - start))
            for at in range(0, width, 256):
                cols = pl.ds(at, min(256, width - at))
                dst[rows, cols] = contract_rows(left[:, rows], right[:, cols]).astype(dst.dtype)
            pltpu.make_async_copy(dst.at[rows], outs[j].at[rows], osem.at[j]).start()
    for j in range(len(jobs)):
        pltpu.make_async_copy(made[j], outs[j], osem.at[j]).wait()


def gradient_call(arrays, loss, jobs, students):
    shape = jax.ShapeDtypeStruct
    outs = [shape((arrays[a].shape[1], arrays[b].shape[1]), jnp.bfloat16) for a, b in jobs]
    smem = pl.BlockSpec(memory_space=pltpu.SMEM)
    scratch = [pltpu.VMEM(item.shape, item.dtype) for item in (*arrays, *outs)]
    scratch += [pltpu.SemaphoreType.DMA((len(arrays),)), pltpu.SemaphoreType.DMA((len(jobs),))]
    return pl.pallas_call(
        functools.partial(gradient_kernel, jobs),
        out_shape=outs + [shape((students,), jnp.float32)],
        in_specs=[ANY] * len(arrays) + [smem],
        out_specs=[ANY] * len(jobs) + [smem],
        scratch_shapes=scratch,
        compiler_params=pltpu.CompilerParams(vmem_limit_bytes=GRANT),
    )(*arrays, loss)


def per_device_kernels(
    mp,
    tokens,
    lengths,
    teacher_gate,
    teacher_up,
    teacher_down,
    first_gate,
    first_up,
    first_down,
    second_gate,
    second_up,
    second_down,
):
    weights, flips = [], []
    for w in (first_gate, first_up, second_gate, second_up, teacher_gate, teacher_up):
        flip = w.shape[1] % 128 != 0
        flips.append(flip)
        weights.append(w.T if flip else w)
    *arrays, loss = layer_call(
        mp, tokens, lengths, weights, (first_down, second_down, teacher_down), tuple(flips)
    )
    jobs = [(1, 3), (2, 4)]
    jobs += [(5 + i, 0) if flips[i] else (0, 5 + i) for i in range(4)]
    made = gradient_call(arrays, loss, tuple(jobs), 2)
    ins = [out.T if flip else out for out, flip in zip(made[2:6], flips)]
    return ins[0], ins[1], made[0], ins[2], ins[3], made[1], made[6]


def per_device(
    tokens,
    lengths,
    teacher_gate,
    teacher_up,
    teacher_down,
    first_gate,
    first_up,
    first_down,
    second_gate,
    second_up,
    second_down,
):
    gathered = lax.all_gather(tokens, "mp", axis=0, tiled=True)
    total_rows = gathered.shape[0]

    def project(weight):
        return jnp.dot(gathered, weight, preferred_element_type=jnp.float32)

    partials = (
        project(teacher_gate),
        project(teacher_up),
        project(first_gate),
        project(first_up),
        project(second_gate),
        project(second_up),
    )
    values = lax.psum(
        (partials[0], partials[1], partials[2], partials[3], partials[4], partials[5]), "split"
    )
    hidden = (
        activate(values[0], values[1]),
        activate(values[2], values[3]),
        activate(values[4], values[5]),
    )
    target = jnp.dot(hidden[0], teacher_down, preferred_element_type=jnp.float32)
    diffs = (
        jnp.dot(hidden[1], first_down, preferred_element_type=jnp.float32) - target,
        jnp.dot(hidden[2], second_down, preferred_element_type=jnp.float32) - target,
    )
    counted = jnp.sum(lengths).astype(jnp.float32)
    summed = lax.psum((diffs[0], diffs[1]), "mp")
    mask = valid_rows(lengths, total_rows)
    partial_loss = (
        jnp.stack([jnp.sum(mask * summed[0] * summed[0]), jnp.sum(mask * summed[1] * summed[1])])
        / counted
    )
    losses = lax.psum(partial_loss, "split")
    cotangents = (
        (2.0 * mask * summed[0] / counted).astype(jnp.bfloat16),
        (2.0 * mask * summed[1] / counted).astype(jnp.bfloat16),
    )
    grad_first_down = contract_rows(hidden[1], cotangents[0]).astype(jnp.bfloat16)
    grad_second_down = contract_rows(hidden[2], cotangents[1]).astype(jnp.bfloat16)
    dims = (((1,), (1,)), ((), ()))
    backs = (
        lax.dot_general(cotangents[0], first_down, dims, preferred_element_type=jnp.float32),
        lax.dot_general(cotangents[1], second_down, dims, preferred_element_type=jnp.float32),
    )
    back_full = lax.psum((backs[0], backs[1]), "split")
    first_dg, first_du = hidden_grads(back_full[0], values[2], values[3])
    second_dg, second_du = hidden_grads(back_full[1], values[4], values[5])
    grads_in = (first_dg, first_du, second_dg, second_du)
    outputs = tuple((contract_rows(gathered, item).astype(jnp.bfloat16) for item in grads_in))
    return (
        outputs[0],
        outputs[1],
        grad_first_down,
        outputs[2],
        outputs[3],
        grad_second_down,
        losses,
    )


def run(mp, split, *args):
    rows = args[0].shape[0] * mp
    if split == 4 and mp == 4 and args[0].shape[0] % 16 == 0 and rows % 64 == 0:
        return per_device_kernels(mp, *args)
    return per_device(*args)


def solution(mesh):
    placed = (
        P(("parts", "mp"), "split"),
        P("parts"),
        P(("parts", "split"), "mp"),
        P(("parts", "split"), "mp"),
        P(("parts", "mp"), "split"),
        P(("parts", "split"), "mp"),
        P(("parts", "split"), "mp"),
        P(("parts", "mp"), "split"),
        P(("parts", "split"), "mp"),
        P(("parts", "split"), "mp"),
        P(("parts", "mp"), "split"),
    )
    return jax.shard_map(
        functools.partial(run, mesh.shape["mp"], mesh.shape["split"]),
        mesh=mesh,
        in_specs=placed,
        out_specs=(
            P(("parts", "split"), "mp"),
            P(("parts", "split"), "mp"),
            P(("parts", "mp"), "split"),
            P(("parts", "split"), "mp"),
            P(("parts", "split"), "mp"),
            P(("parts", "mp"), "split"),
            P("parts"),
        ),
        check_vma=False,
    )
```
